32 devices in a mesh: grp: 2 (over y), tm: 4 (over z), height: 2 (over core), head: 2 (over x).
Axes of the slice: x: 2, y: 2, z: 4, core: 2. Of those that a mesh axis runs over, the one named last changes fastest.
Arguments:
- query_video: bfloat16 [32, 16, 16, 3072], P('grp', 'height', 'tm', 'head'), parts along dimension 0, may hold values from -20 to 20
- key_video: bfloat16 [32, 16, 16, 3072], P('grp', 'height', 'tm', 'head'), parts along dimension 0, may hold values from -20 to 20
- value_video: bfloat16 [32, 16, 16, 3072], P('grp', 'height', 'tm', 'head'), parts along dimension 0, may hold values from -6 to 6
- query_text: bfloat16 [512, 3072], P('grp', 'head'), parts along dimension 0, may hold values from -20 to 20
- key_text: bfloat16 [512, 3072], P('grp', 'head'), parts along dimension 0, may hold values from -6 to 6
- value_text: bfloat16 [512, 3072], P('grp', 'head'), parts along dimension 0, may hold values from -6 to 6
- text_valid: int32 [512], P('grp'), parts along dimension 0, may hold values from 0 to 1, as said below
Outputs:
- out_video: bfloat16 [32, 16, 16, 3072], P('grp', 'height', 'tm', 'head'), parts along dimension 0
- out_text: bfloat16 [512, 3072], P('grp', 'head'), parts along dimension 0
The draws below stay inside these ranges and needn't reach their ends.
There are 2 independent parts, one for each index of `grp`. The reference program is written for one: setup_inputs(seed, part) draws one part's arguments, and reference() takes and returns one part's arrays. A program takes and returns all parts, laid end to end along the dimension named above; each array names one. Nothing has to cross between parts.
Inputs may be any that keep to these rules, and one draw needn't show every extreme that they name: `text_valid`: 1 on a leading run of at least 64 positions and 0 on the rest; at least one position is 0.
All inputs are finite; a program needn't handle non-finite values.
Results may differ from the reference program's by a relative error of at most 0.0037.
Values may be sent and summed in bfloat16 or wider, within the bound.
No kernel may reach another device: no remote copies, remote signals or barrier semaphores. Data moves between devices by JAX's collectives and lax.ppermute only.
A program may use at most 192 MiB of HBM per device.

```python
import math
import jax
import jax.numpy as jnp
from jax import lax

HEADS = 24
HD = 128
TILE = 4
TEXT = 256
FRAMES = 16
ROWS = 16
COLS = 16
FEAT = 3072


def background(key, shape):
    values = jnp.clip(jax.random.normal(key, shape, jnp.float32), -4.0, 4.0) * 1.5
    return values


def draw_query_video(key, part):
    values = background(jax.random.fold_in(key, 1), (FRAMES, ROWS, COLS, HEADS * HD))
    return values.astype(jnp.bfloat16)


def draw_key_video(key, part):
    values = background(jax.random.fold_in(key, 2), (FRAMES, ROWS, COLS, HEADS * HD))
    return values.astype(jnp.bfloat16)


def draw_query_text(key, part):
    values = background(jax.random.fold_in(key, 3), (TEXT, HEADS * HD))
    return values.astype(jnp.bfloat16)


def draw_text_valid(key, part):
    length = jax.random.randint(jax.random.fold_in(key, 21), (), TEXT // 4, TEXT)
    return (jnp.arange(TEXT, dtype=jnp.int32) < length).astype(jnp.int32)


def steps_of(stream_key, extent, shards, least, largest):
    loudness = 1.0
    for axis_at, shards_of in shards:
        heights = jax.random.uniform(jax.random.fold_in(jax.random.fold_in(stream_key, 6), axis_at), (shards_of,), jnp.float32, least / len(shards), largest / len(shards))
        loudness = loudness * jnp.repeat(jnp.exp(heights), extent[axis_at] // shards_of).reshape((-1,) + (1,) * (len(extent) - 1 - axis_at))
    return loudness


def centred(own_key, shape, scale, bound, split=(), kind=jnp.bfloat16):
    array = jax.random.normal(own_key, shape, jnp.float32) * scale
    if len(split) > 0:
        array = steps_of(own_key, shape, split, -0.22, 0.18) * array
    return jnp.clip(array, min=-bound, max=bound).astype(kind)


def setup_inputs(seed: int = 0, part: int = 0) -> dict:
    splits = jax.random.split(jax.random.key(seed), 8)
    own_keys = jax.random.split(jax.random.fold_in(splits[7], part), 8)
    query_video = draw_query_video(jax.random.fold_in(jax.random.fold_in(splits[7], part), 71), part)
    key_video = draw_key_video(jax.random.fold_in(jax.random.fold_in(splits[7], part), 71), part)
    value_video = centred(own_keys[2], (FRAMES, ROWS, COLS, FEAT), 1.0, 6.0, ((1, 2), (2, 4), (3, 2)))
    query_text = draw_query_text(jax.random.fold_in(jax.random.fold_in(splits[7], part), 71), part)
    key_text = centred(own_keys[4], (TEXT, FEAT), 1.5, 6.0, ((1, 2),))
    value_text = centred(own_keys[5], (TEXT, FEAT), 1.0, 6.0, ((1, 2),))
    text_valid = draw_text_valid(jax.random.fold_in(jax.random.fold_in(splits[7], part), 71), part)
    return dict(query_video=query_video, key_video=key_video, value_video=value_video, query_text=query_text, key_text=key_text, value_text=value_text, text_valid=text_valid)


def into_tiles(field):
    time_tiles = field.shape[0] // TILE
    row_tiles = field.shape[1] // TILE
    col_tiles = field.shape[2] // TILE
    shaped = field.reshape(time_tiles, TILE, row_tiles, TILE, col_tiles, TILE, field.shape[3])
    shaped = shaped.transpose(0, 2, 4, 1, 3, 5, 6)
    return shaped.reshape(time_tiles, row_tiles, col_tiles, TILE ** 3, field.shape[3])

def rounded(values):
    return lax.optimization_barrier(values.astype(jnp.bfloat16)).astype(jnp.float32)

def reference(query_video, key_video, value_video, query_text, key_text, value_text, text_valid):
    time_tiles = FRAMES // TILE
    row_tiles = ROWS // TILE
    col_tiles = COLS // TILE
    tile_count = time_tiles * row_tiles * col_tiles
    volume = TILE ** 3
    features = HEADS * HD
    scale_factor = 1.0 / math.sqrt(HD)
    query_tiles = into_tiles(query_video).reshape(tile_count, volume, HEADS, HD).transpose(2, 0, 1, 3)
    pad_spec = ((1, 1), (1, 1), (1, 1), (0, 0), (0, 0))
    key_padded = jnp.pad(into_tiles(key_video), pad_spec).reshape(-1, volume, HEADS, HD).transpose(2, 0, 1, 3)
    value_padded = jnp.pad(into_tiles(value_video), pad_spec).reshape(-1, volume, HEADS, HD).transpose(2, 0, 1, 3)
    key_flat = key_video.reshape(-1, HEADS, HD).transpose(1, 0, 2)
    value_flat = value_video.reshape(-1, HEADS, HD).transpose(1, 0, 2)
    text_queries = query_text.reshape(TEXT, HEADS, HD).transpose(1, 0, 2)
    text_keys = key_text.reshape(TEXT, HEADS, HD).transpose(1, 0, 2)
    text_values = value_text.reshape(TEXT, HEADS, HD).transpose(1, 0, 2)
    slot_ids = jnp.arange(27, dtype=jnp.int32)[None, :]
    numbering = jnp.arange(tile_count, dtype=jnp.int32)
    tile_time = numbering // (row_tiles * col_tiles)
    tile_row = numbering // col_tiles % row_tiles
    tile_col = numbering % col_tiles
    target_time = tile_time[:, None] + slot_ids // 9 - 1
    target_row = tile_row[:, None] + slot_ids // 3 % 3 - 1
    target_col = tile_col[:, None] + slot_ids % 3 - 1
    inside = (target_time >= 0) & (target_time < time_tiles) & (target_row >= 0) & (target_row < row_tiles)
    inside = inside & (target_col >= 0) & (target_col < col_tiles)
    source = ((target_time + 1) * (row_tiles + 2) + target_row + 1) * (col_tiles + 2) + target_col + 1
    source = source.astype(jnp.int32)
    text_open = text_valid > 0

    def per_head(operands):
        head_query, head_keys, head_values, flat_keys, flat_values, text_query, text_key, text_value = operands
        gathered_keys = head_keys[source].astype(jnp.float32)
        gathered_values = head_values[source].astype(jnp.float32)
        video_scores = jnp.einsum('qad,qsbd->qasb', head_query.astype(jnp.float32), gathered_keys) * scale_factor
        video_scores = jnp.where(inside[:, None, :, None], video_scores, -jnp.inf)
        cross_scores = jnp.einsum('qad,kd->qak', head_query.astype(jnp.float32), text_key.astype(jnp.float32)) * scale_factor
        cross_scores = jnp.where(text_open[None, None, :], cross_scores, -jnp.inf)
        video_peak = jnp.maximum(lax.optimization_barrier(jnp.max(video_scores, axis=(2, 3))), lax.optimization_barrier(jnp.max(cross_scores, axis=2)))
        video_probs = jnp.exp(video_scores - video_peak[:, :, None, None])
        cross_probs = jnp.exp(cross_scores - video_peak[:, :, None])
        video_total = lax.optimization_barrier(jnp.sum(video_probs, axis=(2, 3))) + lax.optimization_barrier(jnp.sum(cross_probs, axis=2))
        summed = jnp.einsum('qasb,qsbd->qad', rounded(video_probs), gathered_values)
        summed = summed + jnp.einsum('qak,kd->qad', rounded(cross_probs), text_value.astype(jnp.float32))
        video_out = (summed / video_total[:, :, None]).astype(jnp.bfloat16)
        far_scores = jnp.einsum('kd,nd->kn', text_query.astype(jnp.float32), flat_keys.astype(jnp.float32)) * scale_factor
        near_scores = jnp.einsum('kd,jd->kj', text_query.astype(jnp.float32), text_key.astype(jnp.float32)) * scale_factor
        near_scores = jnp.where(text_open[None, :], near_scores, -jnp.inf)
        text_peak = jnp.maximum(lax.optimization_barrier(jnp.max(far_scores, axis=1)), lax.optimization_barrier(jnp.max(near_scores, axis=1)))
        far_probs = jnp.exp(far_scores - text_peak[:, None])
        near_probs = jnp.exp(near_scores - text_peak[:, None])
        text_total = lax.optimization_barrier(jnp.sum(far_probs, axis=1)) + lax.optimization_barrier(jnp.sum(near_probs, axis=1))
        text_summed = jnp.dot(rounded(far_probs), flat_values.astype(jnp.float32))
        text_summed = text_summed + jnp.dot(rounded(near_probs), text_value.astype(jnp.float32))
        text_out = (text_summed / text_total[:, None]).astype(jnp.bfloat16)
        return (video_out, text_out)
    video_heads, text_heads = lax.map(per_head, (query_tiles, key_padded, value_padded, key_flat, value_flat, text_queries, text_keys, text_values))
    video_heads = video_heads.transpose(1, 2, 0, 3).reshape(time_tiles, row_tiles, col_tiles, TILE, TILE, TILE, features)
    out_video = video_heads.transpose(0, 3, 1, 4, 2, 5, 6).reshape(FRAMES, ROWS, COLS, features)
    out_text = text_heads.transpose(1, 0, 2).reshape(TEXT, features)
    return (out_video, out_text)
```

```python
import functools
import math

import jax
import jax.numpy as jnp
from jax import lax
from jax.experimental import pallas as pl
from jax.experimental.pallas import tpu as pltpu
from jax.sharding import PartitionSpec as P

HD = 128
TILE = 4
VOL = TILE**3
BF16 = jnp.bfloat16
F32 = jnp.float32
SCALE = 1.0 / math.sqrt(HD)
SCALE_2 = SCALE * math.log2(math.e)
VMEM = 63 << 20
THIRD = 32


def cost(microseconds):
    return pl.CostEstimate(flops=int(microseconds * 1.15e9), bytes_accessed=1, transcendentals=0)


def head_groups(heads):
    if heads % 6:
        return [(start, 1) for start in range(heads)]
    unit = heads // 6
    return [(4 * unit, unit), (0, 2 * unit), (2 * unit, 2 * unit), (5 * unit, unit)]


def dot_nt(a, b):
    return lax.dot_general(a, b, (((1,), (1,)), ((), ())), preferred_element_type=F32)


def dot_nn(a, b):
    return lax.dot_general(a, b, (((1,), (0,)), ((), ())), preferred_element_type=F32)


def weigh(p, v):
    return dot_nn(p.astype(BF16), jnp.concatenate([v, jnp.ones_like(v)], axis=1))


def pack_body(scal, k_ref, v_ref, *rest):
    kv_ref = rest[-1] if len(rest) == 1 else rest[2]
    for which, ref in enumerate((k_ref, v_ref)):
        for head in range(kv_ref.shape[1]):
            lanes = slice(head * HD, (head + 1) * HD)
            for r in range(ref.shape[1] // TILE):
                kv_ref[which, head, 0, r] = ref[:, r * TILE : (r + 1) * TILE, :, lanes].reshape(VOL, HD)
    if len(rest) > 1:
        rest[3][...] = rest[0][...]
        rest[4][...] = rest[1][...]


def pack_group(scal, key_video, value_video, start, count, give):
    frames, rows, cols, features = key_video.shape
    time_tiles = frames // TILE
    row_tiles = rows // TILE
    block = pl.BlockSpec((TILE, rows, cols, count * HD), lambda t, s: (t, 0, 0, start // count))
    in_specs = [block, block]
    out_specs = [pl.BlockSpec((2, count, 1, row_tiles, VOL, HD), lambda t, s: (0, 0, t, 0, 0, 0))]
    out_shape = [jax.ShapeDtypeStruct((2, count, time_tiles, row_tiles, VOL, HD), BF16)]
    operands = [key_video, value_video]
    if give:
        in_specs += [pl.BlockSpec((TILE, rows, cols, features // 2), lambda t, s: (t, 0, 0, s[0]))] * 2
        out_specs += [pl.BlockSpec((TILE, rows, cols, features // 2), lambda t, s: (t, 0, 0, 0))] * 2
        out_shape += [jax.ShapeDtypeStruct((frames, rows, cols, features // 2), BF16)] * 2
        operands += [key_video, value_video]
    return pl.pallas_call(
        pack_body,
        grid_spec=pltpu.PrefetchScalarGridSpec(
            num_scalar_prefetch=1, grid=(time_tiles,), in_specs=in_specs, out_specs=out_specs
        ),
        out_shape=out_shape,
        compiler_params=pltpu.CompilerParams(vmem_limit_bytes=VMEM),
        cost_estimate=cost(0),
        name="pack",
    )(scal, *operands)


def video_body(scal, valid_ref, q_ref, own, left, right, edge, edge_left, edge_right, tk_ref, tv_ref, *rest):
    out_ref = rest[-1]
    near = scal[0]
    has_left = scal[1] > 0
    has_right = scal[2] > 0
    time_tiles = q_ref.shape[0] // TILE
    open_keys = valid_ref[...] > 0
    far_rows = pl.ds((1 - near) * TILE, TILE)
    near_rows = pl.ds(near * TILE, TILE)

    def load(ref, which, first, last):
        picked = ref[which, 0, first:last]
        return picked.reshape(picked.shape[0] * picked.shape[1] * VOL, HD)

    def scores(t):
        first = max(t - 1, 0)
        last = min(t + 1, time_tiles - 1) + 1
        frames = slice(t * TILE, (t + 1) * TILE)
        q_far = q_ref[frames, far_rows, :, :].reshape(VOL, HD)
        q_near = q_ref[frames, near_rows, :, :].reshape(VOL, HD)
        q_all = jnp.concatenate([q_far, q_near], axis=0)
        s_text = jnp.where(open_keys, dot_nt(q_all, tk_ref[...]), -jnp.inf)
        wide = [(s_text, None, None)]
        for ref, ok in ((own, None), (left, has_left), (right, has_right)):
            wide.append((dot_nt(q_all, load(ref, 0, first, last)), ref, ok))
        thin = []
        for ref, ok in ((edge, None), (edge_left, has_left), (edge_right, has_right)):
            thin.append((dot_nt(q_near, load(ref, 0, first, last)), ref, ok))
        return first, last, wide, thin

    def peak(entries):
        tops = []
        for s, _, ok in entries:
            top = jnp.max(s, axis=1, keepdims=True)
            tops.append(top if ok is None else jnp.where(ok, top, -jnp.inf))
        return functools.reduce(jnp.maximum, tops)

    def gather(entries, m, first, last):
        summed = None
        for s, ref, ok in entries:
            base = m if ok is None else jnp.where(ok, m, jnp.inf)
            v = tv_ref[...] if ref is None else load(ref, 1, first, last)
            part = weigh(jnp.exp2((s - base) * SCALE_2), v)
            summed = part if summed is None else summed + part
        return summed

    def finish(t, state):
        first, last, wide, thin = state
        frames = slice(t * TILE, (t + 1) * TILE)
        m_all = peak(wide)
        m_near = jnp.maximum(m_all[VOL:], peak(thin))
        m_all = jnp.concatenate([m_all[:VOL], m_near], axis=0)
        summed = gather(wide, m_all, first, last)
        far = summed[:VOL]
        close = summed[VOL:] + gather(thin, m_near, first, last)
        for rows, value in ((far_rows, far), (near_rows, close)):
            out = value[:, :HD] / value[:, HD:]
            out_ref[frames, rows, :, :] = out.astype(BF16).reshape(TILE, TILE, TILE, HD)

    state = scores(0)
    for t in range(time_tiles):
        following = scores(t + 1) if t + 1 < time_tiles else None
        finish(t, state)
        state = following


def video_group(scal, valid, query_video, tiles, key_text, value_text, prior, start, count):
    frames, rows, cols, _ = query_video.shape
    tokens = frames * rows * cols
    time_tiles = frames // TILE
    text = key_text.shape[0]
    head = pl.BlockSpec((frames, rows, cols, HD), lambda i, s: (0, 0, 0, start + i))
    wide = pl.BlockSpec((2, 1, time_tiles, 2, VOL, HD), lambda i, s: (0, i, 0, 0, 0, 0))
    thin = pl.BlockSpec((2, 1, time_tiles, 1, VOL, HD), lambda i, s: (0, i, 0, 1 - s[0], 0, 0))
    word = pl.BlockSpec((text, HD), lambda i, s: (0, start + i))
    specs = [pl.BlockSpec((1, text), lambda i, s: (0, 0)), head, wide, wide, wide, thin, thin, thin, word, word]
    operands = [scal, valid, query_video, *tiles, key_text, value_text]
    aliases = {}
    if prior is not None:
        specs.append(pl.BlockSpec(memory_space=pl.ANY))
        aliases = {len(operands): 0}
        operands.append(prior)
    return pl.pallas_call(
        video_body,
        grid_spec=pltpu.PrefetchScalarGridSpec(
            num_scalar_prefetch=1,
            grid=(count,),
            in_specs=specs,
            out_specs=head,
        ),
        out_shape=jax.ShapeDtypeStruct(query_video.shape, BF16),
        input_output_aliases=aliases,
        compiler_params=pltpu.CompilerParams(vmem_limit_bytes=VMEM),
        cost_estimate=cost(0),
        name="video",
    )(*operands)


def lane_of(shape):
    return lax.broadcasted_iota(jnp.int32, shape, len(shape) - 1)


def send_logs(logs):
    high = logs.astype(BF16).astype(F32)
    mid = (logs - high).astype(BF16).astype(F32)
    low = logs - high - mid
    lane = lane_of(logs.shape)
    whole = jnp.where(lane < THIRD, high, 0.0)
    whole = jnp.where((lane >= THIRD) & (lane < 2 * THIRD), pltpu.roll(mid, THIRD, 1), whole)
    whole = jnp.where((lane >= 2 * THIRD) & (lane < 3 * THIRD), pltpu.roll(low, 2 * THIRD, 1), whole)
    return jnp.where(lane == HD - 1, 1.0, whole).astype(BF16)


def read_logs(sent):
    whole = sent.astype(F32)
    logs = whole + pltpu.roll(whole, HD - THIRD, 1) + pltpu.roll(whole, HD - 2 * THIRD, 1)
    return jnp.where(whole[:, HD - 1 :] > 0, logs, -jnp.inf)


def text_body(scal, valid_ref, q_ref, k_ref, v_ref, k2_ref, v2_ref, tk_ref, tv_ref, sum_ref, log_ref, send_ref):
    at = pl.program_id(0)
    heads = pl.num_programs(0) - 1

    @pl.when(at < heads)
    def _():
        tokens = k_ref.shape[0] * k_ref.shape[1] * k_ref.shape[2]
        q = q_ref[...]
        s_own = dot_nt(q, k_ref[...].reshape(tokens, HD))
        s_pair = dot_nt(q, k2_ref[...].reshape(tokens, HD))
        s_near = jnp.where((valid_ref[...] > 0) & (scal[3] > 0), dot_nt(q, tk_ref[...]), -jnp.inf)
        m = functools.reduce(jnp.maximum, [jnp.max(s, axis=1, keepdims=True) for s in (s_own, s_pair, s_near)])
        both = weigh(jnp.exp2((s_own - m) * SCALE_2), v_ref[...].reshape(tokens, HD))
        both = both + weigh(jnp.exp2((s_pair - m) * SCALE_2), v2_ref[...].reshape(tokens, HD))
        both = both + weigh(jnp.exp2((s_near - m) * SCALE_2), tv_ref[...])
        total = both[:, HD:]
        out = both[:, :HD] / total
        sum_ref[0] = out
        send_ref[0] = out.astype(BF16)
        logs = m * SCALE + jnp.log(total)
        prior = jnp.where(at == 0, 0.0, log_ref[...])
        log_ref[...] = jnp.where(lane_of(logs.shape) == at, logs, prior)

    @pl.when(at == heads)
    def _():
        send_ref[0] = send_logs(log_ref[...])


def text_partial(scal, valid, query_text, key_video, value_video, key_pair, value_pair, key_text, value_text):
    frames, rows, cols, features = key_pair.shape
    heads = features // HD
    text = query_text.shape[0]

    def own_head(i, s):
        return s[4] + jnp.minimum(i, heads - 1)

    word = pl.BlockSpec((text, HD), lambda i, s: (0, own_head(i, s)))
    block = pl.BlockSpec((frames, rows, cols, HD), lambda i, s: (0, 0, 0, own_head(i, s)))
    pair = pl.BlockSpec((frames, rows, cols, HD), lambda i, s: (0, 0, 0, jnp.minimum(i, heads - 1)))
    return pl.pallas_call(
        text_body,
        grid_spec=pltpu.PrefetchScalarGridSpec(
            num_scalar_prefetch=1,
            grid=(heads + 1,),
            in_specs=[pl.BlockSpec((1, text), lambda i, s: (0, 0)), word, block, block, pair, pair, word, word],
            out_specs=[
                pl.BlockSpec((1, text, HD), lambda i, s: (jnp.minimum(i, heads - 1), 0, 0)),
                pl.BlockSpec((text, HD), lambda i, s: (0, 0)),
                pl.BlockSpec((1, text, HD), lambda i, s: (i, 0, 0)),
            ],
        ),
        out_shape=[
            jax.ShapeDtypeStruct((heads, text, HD), F32),
            jax.ShapeDtypeStruct((text, HD), F32),
            jax.ShapeDtypeStruct((heads + 1, text, HD), BF16),
        ],
        compiler_params=pltpu.CompilerParams(vmem_limit_bytes=VMEM),
        cost_estimate=cost(0),
        name="text",
    )(scal, valid, query_text, key_video, value_video, key_pair, value_pair, key_text, value_text)


def combine(parts, heads):
    logs = [part[1] for part in parts]
    top = functools.reduce(jnp.maximum, logs)
    weights = [jnp.exp(log - top) for log in logs]
    total = functools.reduce(jnp.add, weights)
    weights = [weight / total for weight in weights]
    outs = []
    for head in range(heads):
        terms = [weight[:, head : head + 1] * part[0](head) for weight, part in zip(weights, parts)]
        outs.append(functools.reduce(jnp.add, terms))
    return outs, top + jnp.log(total)


def join_body(sum_ref, log_ref, got_ref, out_ref):
    heads = sum_ref.shape[0]
    own = (lambda head: sum_ref[head], log_ref[...])
    got = (lambda head: got_ref[head].astype(F32), read_logs(got_ref[heads]))
    outs, logs = combine([own, got], heads)
    for head in range(heads):
        out_ref[head] = outs[head].astype(BF16)
    out_ref[heads] = send_logs(logs)


def join(sums, logs, got):
    return pl.pallas_call(
        join_body,
        out_shape=jax.ShapeDtypeStruct(got.shape, BF16),
        compiler_params=pltpu.CompilerParams(vmem_limit_bytes=VMEM),
        cost_estimate=cost(0),
        name="join",
    )(sums, logs, got)


def finish_body(scal, own_ref, got_ref, out_ref):
    heads = own_ref.shape[0] - 1
    low = scal[5] > 0
    parts = []
    for flag in (low, jnp.logical_not(low)):

        def pick(index, flag=flag):
            return jnp.where(flag, own_ref[index].astype(F32), got_ref[index].astype(F32))

        parts.append((pick, read_logs(pick(heads))))
    outs, _ = combine(parts, heads)
    for head in range(heads):
        out_ref[:, head * HD : (head + 1) * HD] = outs[head].astype(BF16)


def finish(scal, own, got):
    heads, text, _ = own.shape
    return pl.pallas_call(
        finish_body,
        grid_spec=pltpu.PrefetchScalarGridSpec(
            num_scalar_prefetch=1,
            grid=(1,),
            in_specs=[pl.BlockSpec(own.shape, lambda i, s: (0, 0, 0))] * 2,
            out_specs=pl.BlockSpec((text, (heads - 1) * HD), lambda i, s: (0, 0)),
        ),
        out_shape=jax.ShapeDtypeStruct((text, (heads - 1) * HD), BF16),
        compiler_params=pltpu.CompilerParams(vmem_limit_bytes=VMEM),
        cost_estimate=cost(0),
        name="finish",
    )(scal, own, got)


def after(value, *others):
    return lax.optimization_barrier((value, *others))[0]


def shards(query_video, key_video, value_video, query_text, key_text, value_text, text_valid):
    features = query_video.shape[3]
    heads = features // HD
    strips = lax.axis_size("tm")
    strip = lax.axis_index("tm")
    half = lax.axis_index("height")
    half_heads = heads // 2
    half_features = features // 2

    def swap(array):
        return lax.ppermute(array, "height", [(0, 1), (1, 0)])

    up = [(i, i + 1) for i in range(strips - 1)]
    down = [(i + 1, i) for i in range(strips - 1)]
    scal = jnp.stack(
        [1 - half, strip > 0, strip < strips - 1, strip == 0, half * half_heads, strip < strips // 2]
    ).astype(jnp.int32)
    valid = text_valid.reshape(1, -1)
    groups = head_groups(heads)

    def to_neighbours(own):
        return lax.ppermute(own, "tm", up), lax.ppermute(own, "tm", down)

    owns = []
    edges = []
    pairs = []
    for index, (start, count) in enumerate(groups):
        packed = pack_group(scal, key_video, value_video, start, count, index == 0)
        owns.append(packed[0])
        pairs += packed[1:]
    key_pair, value_pair = swap(pairs[0]), swap(pairs[1])
    edges = [swap(own) for own in owns]
    sums, logs, sent = text_partial(
        scal, valid, query_text, key_video, value_video, key_pair, value_pair, key_text, value_text
    )

    middle = strips // 2
    for step in range(1, middle):
        got = lax.ppermute(sent, "tm", [(step - 1, step), (strips - step, strips - step - 1)])
        sent = join(sums, logs, got)
    got = lax.ppermute(sent, "tm", [(middle - 1, middle), (middle, middle - 1)])
    mine = finish(scal, sent, got)
    for step in range(middle - 1, 0, -1):
        got = lax.ppermute(mine, "tm", [(step, step - 1), (strips - step - 1, strips - step)])
        mine = jnp.where((strip == step - 1) | (strip == strips - step), got, mine)
    other = swap(mine)
    first = half == 0
    out_text = jnp.concatenate([jnp.where(first, mine, other), jnp.where(first, other, mine)], axis=1)

    out_video = None
    sides = [to_neighbours(own) for own in owns[:2]]
    for index, (start, count) in enumerate(groups):
        left, right = sides[index]
        if out_video is not None:
            left, right = after(left, out_video), after(right, out_video)
        edge_left, edge_right = swap(left), swap(right)
        if index + 2 < len(groups):
            sides.append(to_neighbours(after(owns[index + 2], edge_left, edge_right)))
        tiles = (owns[index], left, right, edges[index], edge_left, edge_right)
        out_video = video_group(scal, valid, query_video, tiles, key_text, value_text, out_video, start, count)
    return (out_video, out_text)


def solution(mesh):
    if mesh.shape["height"] != 2 or mesh.shape["tm"] % 2:
        raise ValueError("unsupported mesh")
    placed = (
        P("grp", "height", "tm", "head"),
        P("grp", "height", "tm", "head"),
        P("grp", "height", "tm", "head"),
        P("grp", "head"),
        P("grp", "head"),
        P("grp", "head"),
        P("grp"),
    )
    return jax.shard_map(
        shards,
        mesh=mesh,
        in_specs=placed,
        out_specs=(P("grp", "height", "tm", "head"), P("grp", "head")),
        check_vma=False,
    )
```

```python
import functools
import math

import jax
import jax.numpy as jnp
from jax import lax
from jax.experimental import pallas as pl
from jax.experimental.pallas import tpu as pltpu
from jax.sharding import PartitionSpec as P

HD = 128
TILE = 4
VOL = TILE**3
BF16 = jnp.bfloat16
F32 = jnp.float32
SCALE = 1.0 / math.sqrt(HD)
SCALE_2 = SCALE * math.log2(math.e)
VMEM = 63 << 20
THIRD = 32
SIZES = (3, 3)


def cost(microseconds):
    return pl.CostEstimate(flops=int(microseconds * 1.15e9), bytes_accessed=1, transcendentals=0)


def head_groups(heads):
    sizes = SIZES if heads == sum(SIZES) else [heads - 1, 1]
    starts = [sum(sizes[:i]) for i in range(len(sizes))]
    return list(zip(starts, sizes))


def dot_nt(a, b):
    return lax.dot_general(a, b, (((1,), (1,)), ((), ())), preferred_element_type=F32)


def dot_nn(a, b):
    return lax.dot_general(a, b, (((1,), (0,)), ((), ())), preferred_element_type=F32)


def weigh(p, v):
    return dot_nn(p.astype(BF16), jnp.concatenate([v, jnp.ones_like(v)], axis=1))


def pack_body(sizes, scal, *rest):
    k_ref, v_ref = rest[:2]
    tiles = rest[-len(sizes) - 1 : -1] if len(rest) == len(sizes) + 4 else rest[-len(sizes) :]
    head = 0
    for size, kv_ref in zip(sizes, tiles):
        for at in range(size):
            lanes = slice(head * HD, (head + 1) * HD)
            head += 1
            for which, ref in enumerate((k_ref, v_ref)):
                for r in range(ref.shape[1] // TILE):
                    kv_ref[which, at, 0, r] = ref[:, r * TILE : (r + 1) * TILE, :, lanes].reshape(VOL, HD)
    if len(rest) == len(sizes) + 4:
        rest[-1][...] = rest[2][...]


def pack_half(scal, key_video, value_video, sizes, query_video=None):
    frames, rows, cols, features = key_video.shape
    time_tiles = frames // TILE
    row_tiles = rows // TILE
    theirs = query_video is not None
    block = pl.BlockSpec(
        (TILE, rows, cols, features // 2), lambda t, s: (t, 0, 0, 1 - s[4] if theirs else s[4])
    )
    operands = [key_video, value_video]
    out_specs = [
        pl.BlockSpec((2, size, 1, row_tiles, VOL, HD), lambda t, s: (0, 0, t, 0, 0, 0)) for size in sizes
    ]
    out_shape = [jax.ShapeDtypeStruct((2, size, time_tiles, row_tiles, VOL, HD), BF16) for size in sizes]
    if theirs:
        operands.append(query_video)
        out_specs.append(pl.BlockSpec((TILE, rows, cols, features // 2), lambda t, s: (t, 0, 0, 0)))
        out_shape.append(jax.ShapeDtypeStruct((frames, rows, cols, features // 2), BF16))
    return pl.pallas_call(
        functools.partial(pack_body, sizes),
        grid_spec=pltpu.PrefetchScalarGridSpec(
            num_scalar_prefetch=1, grid=(time_tiles,), in_specs=[block] * len(operands), out_specs=out_specs
        ),
        out_shape=out_shape,
        compiler_params=pltpu.CompilerParams(vmem_limit_bytes=VMEM),
        cost_estimate=cost(0),
        name="pack",
    )(scal, *operands)


def video_body(scal, valid_ref, own_q, pair_q, *rest):
    own_tiles, pair_tiles, (tk_ref, tv_ref) = rest[:3], rest[3:6], rest[6:8]
    own_out, pair_out = rest[-2:]
    has_left = scal[1] > 0
    has_right = scal[2] > 0
    time_tiles = own_q.shape[0] // TILE
    open_keys = valid_ref[...] > 0

    def load(ref, which, first, last, row):
        picked = ref[which, 0, first:last] if row is None else ref[which, 0, first:last, pl.ds(row, 1)]
        return picked.reshape(picked.shape[0] * picked.shape[1] * VOL, HD)

    def scores(step):
        part, t = step
        q_ref = (own_q, pair_q)[part]
        near = scal[0] if part == 0 else 1 - scal[0]
        far_rows = pl.ds((1 - near) * TILE, TILE)
        near_rows = pl.ds(near * TILE, TILE)
        own, left, right = (own_tiles, pair_tiles)[part]
        edge, edge_left, edge_right = (pair_tiles, own_tiles)[part]
        row = 1 - near
        first = max(t - 1, 0)
        last = min(t + 1, time_tiles - 1) + 1
        frames = slice(t * TILE, (t + 1) * TILE)
        q_far = q_ref[frames, far_rows, :, :].reshape(VOL, HD)
        q_near = q_ref[frames, near_rows, :, :].reshape(VOL, HD)
        q_all = jnp.concatenate([q_far, q_near], axis=0)
        s_text = jnp.where(open_keys, dot_nt(q_all, tk_ref[...]), -jnp.inf)
        wide = [(s_text, None, None)]
        for ref, ok in ((own, None), (left, has_left), (right, has_right)):
            wide.append((dot_nt(q_all, load(ref, 0, first, last, None)), ref, ok))
        thin = []
        for ref, ok in ((edge, None), (edge_left, has_left), (edge_right, has_right)):
            thin.append((dot_nt(q_near, load(ref, 0, first, last, row)), ref, ok))
        return first, last, wide, thin, row, far_rows, near_rows

    def peak(entries):
        tops = []
        for s, _, ok in entries:
            top = jnp.max(s, axis=1, keepdims=True)
            tops.append(top if ok is None else jnp.where(ok, top, -jnp.inf))
        return functools.reduce(jnp.maximum, tops)

    def gather(entries, m, first, last, row):
        summed = None
        for s, ref, ok in entries:
            base = m if ok is None else jnp.where(ok, m, jnp.inf)
            v = tv_ref[...] if ref is None else load(ref, 1, first, last, row)
            part = weigh(jnp.exp2((s - base) * SCALE_2), v)
            summed = part if summed is None else summed + part
        return summed

    def finish(step, state):
        part, t = step
        out_ref = (own_out, pair_out)[part]
        first, last, wide, thin, row, far_rows, near_rows = state
        frames = slice(t * TILE, (t + 1) * TILE)
        m_all = peak(wide)
        m_near = jnp.maximum(m_all[VOL:], peak(thin))
        m_all = jnp.concatenate([m_all[:VOL], m_near], axis=0)
        summed = gather(wide, m_all, first, last, None)
        far = summed[:VOL]
        close = summed[VOL:] + gather(thin, m_near, first, last, row)
        for rows, value in ((far_rows, far), (near_rows, close)):
            out = value[:, :HD] / value[:, HD:]
            out_ref[frames, rows, :, :] = out.astype(BF16).reshape(TILE, TILE, TILE, HD)

    steps = [(part, t) for part in range(2) for t in range(time_tiles)]
    state = scores(steps[0])
    for at, step in enumerate(steps):
        following = scores(steps[at + 1]) if at + 1 < len(steps) else None
        finish(step, state)
        state = following


def video_group(scal, valid, query_video, pair_query, mine, pair, key_text, value_text, prior, start, count):
    frames, rows, cols, _ = query_video.shape
    half_heads = pair_query.shape[3] // HD
    time_tiles = frames // TILE
    text = key_text.shape[0]
    block = (frames, rows, cols, HD)
    own_head = pl.BlockSpec(block, lambda i, s: (0, 0, 0, s[4] * half_heads + start + i))
    pair_head = pl.BlockSpec(block, lambda i, s: (0, 0, 0, start + i))
    given = pl.BlockSpec(block, lambda i, s: (0, 0, 0, i))
    of_half = pl.BlockSpec((2, 1, time_tiles, 2, VOL, HD), lambda i, s: (0, start + i, 0, 0, 0, 0))
    of_group = pl.BlockSpec((2, 1, time_tiles, 2, VOL, HD), lambda i, s: (0, i, 0, 0, 0, 0))
    word = pl.BlockSpec((text, HD), lambda i, s: (0, s[4] * half_heads + start + i))
    specs = [pl.BlockSpec((1, text), lambda i, s: (0, 0)), own_head, pair_head]
    specs += [of_half] * 3 + [of_group] * 3 + [word, word]
    operands = [scal, valid, query_video, pair_query, *mine, *pair, key_text, value_text]
    aliases = {}
    if prior is not None:
        specs.append(pl.BlockSpec(memory_space=pl.ANY))
        aliases = {len(operands): 0}
        operands.append(prior)
    return pl.pallas_call(
        video_body,
        grid_spec=pltpu.PrefetchScalarGridSpec(
            num_scalar_prefetch=1,
            grid=(count,),
            in_specs=specs,
            out_specs=[own_head, given],
        ),
        out_shape=[
            jax.ShapeDtypeStruct(query_video.shape, BF16),
            jax.ShapeDtypeStruct((frames, rows, cols, count * HD), BF16),
        ],
        input_output_aliases=aliases,
        compiler_params=pltpu.CompilerParams(vmem_limit_bytes=VMEM),
        cost_estimate=cost(0),
        name="video",
    )(*operands)


def lane_of(shape):
    return lax.broadcasted_iota(jnp.int32, shape, len(shape) - 1)


def send_logs(logs):
    high = logs.astype(BF16).astype(F32)
    mid = (logs - high).astype(BF16).astype(F32)
    low = logs - high - mid
    lane = lane_of(logs.shape)
    whole = jnp.where(lane < THIRD, high, 0.0)
    whole = jnp.where((lane >= THIRD) & (lane < 2 * THIRD), pltpu.roll(mid, THIRD, 1), whole)
    whole = jnp.where((lane >= 2 * THIRD) & (lane < 3 * THIRD), pltpu.roll(low, 2 * THIRD, 1), whole)
    return jnp.where(lane == HD - 1, 1.0, whole).astype(BF16)


def read_logs(sent):
    whole = sent.astype(F32)
    logs = whole + pltpu.roll(whole, HD - THIRD, 1) + pltpu.roll(whole, HD - 2 * THIRD, 1)
    return jnp.where(whole[:, HD - 1 :] > 0, logs, -jnp.inf)


def text_body(groups, scal, valid_ref, q_ref, mine_ref, tk_ref, tv_ref, *rest):
    pairs = rest[: len(groups)]
    sum_ref, log_ref, send_ref = rest[len(groups) :]
    at = pl.program_id(0)
    heads = pl.num_programs(0) - 1

    def work(pair_ref):
        q = q_ref[...]

        def tokens(ref, which):
            whole = ref[which, 0]
            return whole.reshape(whole.shape[0] * whole.shape[1] * VOL, HD)

        def scores(rows):
            near = jnp.where((valid_ref[...] > 0) & (scal[3] > 0), dot_nt(q[rows], tk_ref[...]), -jnp.inf)
            return [dot_nt(q[rows], tokens(mine_ref, 0)), dot_nt(q[rows], tokens(pair_ref, 0)), near]

        def reduce(rows, parts):
            m = functools.reduce(jnp.maximum, [jnp.max(s, axis=1, keepdims=True) for s in parts])
            values = (tokens(mine_ref, 1), tokens(pair_ref, 1), tv_ref[...])
            both = functools.reduce(
                jnp.add, [weigh(jnp.exp2((s - m) * SCALE_2), v) for s, v in zip(parts, values)]
            )
            total = both[:, HD:]
            out = both[:, :HD] / total
            sum_ref[0, rows] = out
            send_ref[0, rows] = out.astype(BF16)
            logs = m * SCALE + jnp.log(total)
            prior = jnp.where(at == 0, 0.0, log_ref[rows])
            log_ref[rows] = jnp.where(lane_of(logs.shape) == at, logs, prior)

        size = q.shape[0] // 2
        low, high = slice(0, size), slice(size, 2 * size)
        first = scores(low)
        second = scores(high)
        reduce(low, first)
        reduce(high, second)

    for (start, count), pair_ref in zip(groups, pairs):
        pl.when((at >= start) & (at < start + count))(functools.partial(work, pair_ref))

    @pl.when(at == heads)
    def _():
        send_ref[0] = send_logs(log_ref[...])


def text_partial(scal, valid, query_text, mine, pairs, groups, key_text, value_text):
    _, heads, time_tiles, _, _, _ = mine.shape
    text = query_text.shape[0]
    block = (2, 1, time_tiles, 2, VOL, HD)

    def of_group(start, count):
        return pl.BlockSpec(block, lambda i, s: (0, jnp.clip(i - start, 0, count - 1), 0, 0, 0, 0))

    word = pl.BlockSpec((text, HD), lambda i, s: (0, s[4] * heads + jnp.minimum(i, heads - 1)))
    return pl.pallas_call(
        functools.partial(text_body, groups),
        grid_spec=pltpu.PrefetchScalarGridSpec(
            num_scalar_prefetch=1,
            grid=(heads + 1,),
            in_specs=[pl.BlockSpec((1, text), lambda i, s: (0, 0)), word, of_group(0, heads), word, word]
            + [of_group(start, count) for start, count in groups],
            out_specs=[
                pl.BlockSpec((1, text, HD), lambda i, s: (jnp.minimum(i, heads - 1), 0, 0)),
                pl.BlockSpec((text, HD), lambda i, s: (0, 0)),
                pl.BlockSpec((1, text, HD), lambda i, s: (i, 0, 0)),
            ],
        ),
        out_shape=[
            jax.ShapeDtypeStruct((heads, text, HD), F32),
            jax.ShapeDtypeStruct((text, HD), F32),
            jax.ShapeDtypeStruct((heads + 1, text, HD), BF16),
        ],
        compiler_params=pltpu.CompilerParams(vmem_limit_bytes=VMEM),
        cost_estimate=cost(0),
        name="text",
    )(scal, valid, query_text, mine, key_text, value_text, *pairs)


def combine(parts, heads):
    logs = [part[1] for part in parts]
    top = functools.reduce(jnp.maximum, logs)
    weights = [jnp.exp(log - top) for log in logs]
    total = functools.reduce(jnp.add, weights)
    weights = [weight / total for weight in weights]
    outs = []
    for head in range(heads):
        terms = [weight[:, head : head + 1] * part[0](head) for weight, part in zip(weights, parts)]
        outs.append(functools.reduce(jnp.add, terms))
    return outs, top + jnp.log(total)


def join_body(sum_ref, log_ref, got_ref, out_ref):
    heads = sum_ref.shape[0]
    own = (lambda head: sum_ref[head], log_ref[...])
    got = (lambda head: got_ref[head].astype(F32), read_logs(got_ref[heads]))
    outs, logs = combine([own, got], heads)
    for head in range(heads):
        out_ref[head] = outs[head].astype(BF16)
    out_ref[heads] = send_logs(logs)


def join(sums, logs, got):
    return pl.pallas_call(
        join_body,
        out_shape=jax.ShapeDtypeStruct(got.shape, BF16),
        compiler_params=pltpu.CompilerParams(vmem_limit_bytes=VMEM),
        cost_estimate=cost(0),
        name="join",
    )(sums, logs, got)


def finish_body(scal, own_ref, got_ref, out_ref):
    heads = own_ref.shape[0] - 1
    low = scal[5] > 0
    parts = []
    for flag in (low, jnp.logical_not(low)):

        def pick(index, flag=flag):
            return jnp.where(flag, own_ref[index].astype(F32), got_ref[index].astype(F32))

        parts.append((pick, read_logs(pick(heads))))
    outs, _ = combine(parts, heads)
    for head in range(heads):
        out_ref[:, head * HD : (head + 1) * HD] = outs[head].astype(BF16)


def finish(scal, own, got):
    heads, text, _ = own.shape
    return pl.pallas_call(
        finish_body,
        grid_spec=pltpu.PrefetchScalarGridSpec(
            num_scalar_prefetch=1,
            grid=(1,),
            in_specs=[pl.BlockSpec(own.shape, lambda i, s: (0, 0, 0))] * 2,
            out_specs=pl.BlockSpec((text, (heads - 1) * HD), lambda i, s: (0, 0)),
        ),
        out_shape=jax.ShapeDtypeStruct((text, (heads - 1) * HD), BF16),
        compiler_params=pltpu.CompilerParams(vmem_limit_bytes=VMEM),
        cost_estimate=cost(0),
        name="finish",
    )(scal, own, got)


def after(value, *others):
    return lax.optimization_barrier((value, *others))[0]


def shards(query_video, key_video, value_video, query_text, key_text, value_text, text_valid):
    features = query_video.shape[3]
    heads = features // HD
    strips = lax.axis_size("tm")
    strip = lax.axis_index("tm")
    half = lax.axis_index("height")
    half_heads = heads // 2

    def swap(array):
        return lax.ppermute(array, "height", [(0, 1), (1, 0)])

    up = [(i, i + 1) for i in range(strips - 1)]
    down = [(i + 1, i) for i in range(strips - 1)]
    scal = jnp.stack(
        [1 - half, strip > 0, strip < strips - 1, strip == 0, half, strip < strips // 2]
    ).astype(jnp.int32)
    valid = text_valid.reshape(1, -1)
    groups = head_groups(half_heads)

    def to_neighbours(array):
        return lax.ppermute(array, "tm", up), lax.ppermute(array, "tm", down)

    (mine,) = pack_half(scal, key_video, value_video, (half_heads,))
    mine_sides = to_neighbours(mine)
    theirs = pack_half(after(scal, mine), key_video, value_video, [count for _, count in groups], query_video)
    pairs = [swap(array) for array in theirs[:-1]]
    pair_query = swap(theirs[-1])
    sums, logs, sent = text_partial(after(scal, pair_query), valid, query_text, mine, pairs, groups, key_text, value_text)

    middle = strips // 2
    for step in range(1, middle):
        got = lax.ppermute(sent, "tm", [(step - 1, step), (strips - step, strips - step - 1)])
        sent = join(sums, after(logs, *mine_sides), got)
    got = lax.ppermute(sent, "tm", [(middle - 1, middle), (middle, middle - 1)])

    def place(whole, part, start):
        column = ((1 - half) * half_heads + start) * HD
        return lax.dynamic_update_slice_in_dim(whole, part, column, 3)

    out_video = None
    waiting = []
    for index, (start, count) in enumerate(groups):
        pair = (pairs[index], *to_neighbours(pairs[index]))
        out_video, given = video_group(
            scal, valid, query_video, pair_query, (mine, *mine_sides), pair, key_text, value_text, out_video, start, count
        )
        if index == 0:
            opened = after(scal, out_video)
        for part in waiting:
            out_video = place(out_video, *part)
        waiting = [(swap(given), start)]
    for part in waiting:
        out_video = place(out_video, *part)

    done = finish(opened, sent, got)
    for step in range(middle - 1, 0, -1):
        got = lax.ppermute(done, "tm", [(step, step - 1), (strips - step - 1, strips - step)])
        done = jnp.where((strip == step - 1) | (strip == strips - step), got, done)
    other = swap(done)
    first = half == 0
    out_text = jnp.concatenate([jnp.where(first, done, other), jnp.where(first, other, done)], axis=1)
    return (out_video, out_text)


def solution(mesh):
    if mesh.shape["height"] != 2 or mesh.shape["tm"] % 2:
        raise ValueError("unsupported mesh")
    placed = (
        P("grp", "height", "tm", "head"),
        P("grp", "height", "tm", "head"),
        P("grp", "height", "tm", "head"),
        P("grp", "head"),
        P("grp", "head"),
        P("grp", "head"),
        P("grp"),
    )
    return jax.shard_map(
        shards,
        mesh=mesh,
        in_specs=placed,
        out_specs=(P("grp", "height", "tm", "head"), P("grp", "head")),
        check_vma=False,
    )
```

```python
import functools
import math

import jax
import jax.numpy as jnp
from jax import lax
from jax.experimental import pallas as pl
from jax.experimental.pallas import tpu as pltpu
from jax.sharding import PartitionSpec as P

HD = 128
TILE = 4
VOL = TILE**3
BF16 = jnp.bfloat16
F32 = jnp.float32
SCALE = 1.0 / math.sqrt(HD)
SCALE_2 = SCALE * math.log2(math.e)
VMEM = 255 << 18
THIRD = 32
SIZES = (3, 3)


def cost(microseconds):
    return pl.CostEstimate(flops=int(microseconds * 1.15e9), bytes_accessed=1, transcendentals=0)


def head_groups(heads):
    sizes = SIZES if heads == sum(SIZES) else [heads - 1, 1]
    starts = [sum(sizes[:i]) for i in range(len(sizes))]
    return list(zip(starts, sizes))


def dot_nt(a, b):
    return lax.dot_general(a, b, (((1,), (1,)), ((), ())), preferred_element_type=F32)


def dot_nn(a, b):
    return lax.dot_general(a, b, (((1,), (0,)), ((), ())), preferred_element_type=F32)


def weigh(p, v):
    return dot_nn(p.astype(BF16), jnp.concatenate([v, jnp.ones_like(v)], axis=1))


def pack_body(sizes, scal, *rest):
    k_ref, v_ref = rest[:2]
    tiles = rest[-len(sizes) - 1 : -1] if len(rest) == len(sizes) + 4 else rest[-len(sizes) :]
    head = 0
    for size, kv_ref in zip(sizes, tiles):
        for at in range(size):
            lanes = slice(head * HD, (head + 1) * HD)
            head += 1
            for which, ref in enumerate((k_ref, v_ref)):
                for t in range(ref.shape[0] // TILE):
                    frames = slice(t * TILE, (t + 1) * TILE)
                    for r in range(ref.shape[1] // TILE):
                        tile = ref[frames, r * TILE : (r + 1) * TILE, :, lanes]
                        kv_ref[which, at, t, r] = tile.reshape(VOL, HD)
    if len(rest) == len(sizes) + 4:
        rest[-1][...] = rest[2][...]


def pack_half(scal, key_video, value_video, sizes, query_video=None):
    frames, rows, cols, features = key_video.shape
    time_tiles = frames // TILE
    row_tiles = rows // TILE
    theirs = query_video is not None
    depth = 2 if time_tiles % 2 == 0 else 1
    block = pl.BlockSpec(
        (depth * TILE, rows, cols, features // 2), lambda t, s: (t, 0, 0, 1 - s[4] if theirs else s[4])
    )
    operands = [key_video, value_video]
    out_specs = [
        pl.BlockSpec((2, size, depth, row_tiles, VOL, HD), lambda t, s: (0, 0, t, 0, 0, 0)) for size in sizes
    ]
    out_shape = [jax.ShapeDtypeStruct((2, size, time_tiles, row_tiles, VOL, HD), BF16) for size in sizes]
    if theirs:
        operands.append(query_video)
        out_specs.append(pl.BlockSpec((depth * TILE, rows, cols, features // 2), lambda t, s: (t, 0, 0, 0)))
        out_shape.append(jax.ShapeDtypeStruct((frames, rows, cols, features // 2), BF16))
    return pl.pallas_call(
        functools.partial(pack_body, sizes),
        grid_spec=pltpu.PrefetchScalarGridSpec(
            num_scalar_prefetch=1, grid=(time_tiles // depth,), in_specs=[block] * len(operands), out_specs=out_specs
        ),
        out_shape=out_shape,
        compiler_params=pltpu.CompilerParams(vmem_limit_bytes=VMEM),
        cost_estimate=cost(0),
        name="pack",
    )(scal, *operands)


def video_body(scal, valid_ref, own_q, pair_q, *rest):
    own_tiles, pair_tiles, (tk_ref, tv_ref) = rest[:3], rest[3:6], rest[6:8]
    own_out, pair_out = rest[-2:]
    has_left = scal[1] > 0
    has_right = scal[2] > 0
    time_tiles = own_q.shape[0] // TILE
    open_keys = valid_ref[...] > 0

    def load(ref, which, first, last, row):
        picked = ref[which, 0, first:last] if row is None else ref[which, 0, first:last, pl.ds(row, 1)]
        return picked.reshape(picked.shape[0] * picked.shape[1] * VOL, HD)

    def scores(step):
        part, t = step
        q_ref = (own_q, pair_q)[part]
        near = scal[0] if part == 0 else 1 - scal[0]
        far_rows = pl.ds((1 - near) * TILE, TILE)
        near_rows = pl.ds(near * TILE, TILE)
        own, left, right = (own_tiles, pair_tiles)[part]
        edge, edge_left, edge_right = (pair_tiles, own_tiles)[part]
        row = 1 - near
        first = max(t - 1, 0)
        last = min(t + 1, time_tiles - 1) + 1
        frames = slice(t * TILE, (t + 1) * TILE)
        q_far = q_ref[frames, far_rows, :, :].reshape(VOL, HD)
        q_near = q_ref[frames, near_rows, :, :].reshape(VOL, HD)
        q_all = jnp.concatenate([q_far, q_near], axis=0)
        s_text = jnp.where(open_keys, dot_nt(q_all, tk_ref[...]), -jnp.inf)
        wide = [(s_text, None, None)]
        for ref, ok in ((own, None), (left, has_left), (right, has_right)):
            wide.append((dot_nt(q_all, load(ref, 0, first, last, None)), ref, ok))
        thin = []
        for ref, ok in ((edge, None), (edge_left, has_left), (edge_right, has_right)):
            thin.append((dot_nt(q_near, load(ref, 0, first, last, row)), ref, ok))
        return first, last, wide, thin, row, far_rows, near_rows

    def peak(entries):
        tops = []
        for s, _, ok in entries:
            top = jnp.max(s, axis=1, keepdims=True)
            tops.append(top if ok is None else jnp.where(ok, top, -jnp.inf))
        return functools.reduce(jnp.maximum, tops)

    def gather(entries, m, first, last, row):
        summed = None
        for s, ref, ok in entries:
            base = m if ok is None else jnp.where(ok, m, jnp.inf)
            v = tv_ref[...] if ref is None else load(ref, 1, first, last, row)
            part = weigh(jnp.exp2((s - base) * SCALE_2), v)
            summed = part if summed is None else summed + part
        return summed

    def finish(step, state):
        part, t = step
        out_ref = (own_out, pair_out)[part]
        first, last, wide, thin, row, far_rows, near_rows = state
        frames = slice(t * TILE, (t + 1) * TILE)
        m_all = peak(wide)
        m_near = jnp.maximum(m_all[VOL:], peak(thin))
        m_all = jnp.concatenate([m_all[:VOL], m_near], axis=0)
        summed = gather(wide, m_all, first, last, None)
        far = summed[:VOL]
        close = summed[VOL:] + gather(thin, m_near, first, last, row)
        for rows, value in ((far_rows, far), (near_rows, close)):
            out = value[:, :HD] / value[:, HD:]
            out_ref[frames, rows, :, :] = out.astype(BF16).reshape(TILE, TILE, TILE, HD)

    steps = [(part, t) for part in range(2) for t in range(time_tiles)]
    state = scores(steps[0])
    for at, step in enumerate(steps):
        following = scores(steps[at + 1]) if at + 1 < len(steps) else None
        finish(step, state)
        state = following


def video_group(scal, valid, query_video, pair_query, mine, pair, key_text, value_text, prior, start, count):
    frames, rows, cols, _ = query_video.shape
    half_heads = pair_query.shape[3] // HD
    time_tiles = frames // TILE
    text = key_text.shape[0]
    block = (frames, rows, cols, HD)
    own_head = pl.BlockSpec(block, lambda i, s: (0, 0, 0, s[4] * half_heads + start + i))
    pair_head = pl.BlockSpec(block, lambda i, s: (0, 0, 0, start + i))
    given = pl.BlockSpec(block, lambda i, s: (0, 0, 0, i))
    of_half = pl.BlockSpec((2, 1, time_tiles, 2, VOL, HD), lambda i, s: (0, start + i, 0, 0, 0, 0))
    of_group = pl.BlockSpec((2, 1, time_tiles, 2, VOL, HD), lambda i, s: (0, i, 0, 0, 0, 0))
    word = pl.BlockSpec((text, HD), lambda i, s: (0, s[4] * half_heads + start + i))
    specs = [pl.BlockSpec((1, text), lambda i, s: (0, 0)), own_head, pair_head]
    specs += [of_half] * 3 + [of_group] * 3 + [word, word]
    operands = [scal, valid, query_video, pair_query, *mine, *pair, key_text, value_text]
    aliases = {}
    if prior is not None:
        specs.append(pl.BlockSpec(memory_space=pl.ANY))
        aliases = {len(operands): 0}
        operands.append(prior)
    return pl.pallas_call(
        video_body,
        grid_spec=pltpu.PrefetchScalarGridSpec(
            num_scalar_prefetch=1,
            grid=(count,),
            in_specs=specs,
            out_specs=[own_head, given],
        ),
        out_shape=[
            jax.ShapeDtypeStruct(query_video.shape, BF16),
            jax.ShapeDtypeStruct((frames, rows, cols, count * HD), BF16),
        ],
        input_output_aliases=aliases,
        compiler_params=pltpu.CompilerParams(vmem_limit_bytes=VMEM),
        cost_estimate=cost(0),
        name="video",
    )(*operands)


def lane_of(shape):
    return lax.broadcasted_iota(jnp.int32, shape, len(shape) - 1)


def send_logs(logs):
    high = logs.astype(BF16).astype(F32)
    mid = (logs - high).astype(BF16).astype(F32)
    low = logs - high - mid
    lane = lane_of(logs.shape)
    whole = jnp.where(lane < THIRD, high, 0.0)
    whole = jnp.where((lane >= THIRD) & (lane < 2 * THIRD), pltpu.roll(mid, THIRD, 1), whole)
    whole = jnp.where((lane >= 2 * THIRD) & (lane < 3 * THIRD), pltpu.roll(low, 2 * THIRD, 1), whole)
    return jnp.where(lane == HD - 1, 1.0, whole).astype(BF16)


def read_logs(sent):
    whole = sent.astype(F32)
    logs = whole + pltpu.roll(whole, HD - THIRD, 1) + pltpu.roll(whole, HD - 2 * THIRD, 1)
    return jnp.where(whole[:, HD - 1 :] > 0, logs, -jnp.inf)


def text_body(groups, scal, valid_ref, q_ref, mine_ref, tk_ref, tv_ref, *rest):
    pairs = rest[: len(groups)]
    sum_ref, log_ref, send_ref = rest[len(groups) :]
    at = pl.program_id(0)
    heads = pl.num_programs(0) - 1

    def work(pair_ref):
        q = q_ref[...]

        def tokens(ref, which):
            whole = ref[which, 0]
            return whole.reshape(whole.shape[0] * whole.shape[1] * VOL, HD)

        def scores(rows):
            near = jnp.where((valid_ref[...] > 0) & (scal[3] > 0), dot_nt(q[rows], tk_ref[...]), -jnp.inf)
            return [dot_nt(q[rows], tokens(mine_ref, 0)), dot_nt(q[rows], tokens(pair_ref, 0)), near]

        def reduce(rows, parts):
            m = functools.reduce(jnp.maximum, [jnp.max(s, axis=1, keepdims=True) for s in parts])
            values = (tokens(mine_ref, 1), tokens(pair_ref, 1), tv_ref[...])
            both = functools.reduce(
                jnp.add, [weigh(jnp.exp2((s - m) * SCALE_2), v) for s, v in zip(parts, values)]
            )
            total = both[:, HD:]
            out = both[:, :HD] / total
            sum_ref[0, rows] = out
            send_ref[0, rows] = out.astype(BF16)
            logs = m * SCALE + jnp.log(total)
            prior = jnp.where(at == 0, 0.0, log_ref[rows])
            log_ref[rows] = jnp.where(lane_of(logs.shape) == at, logs, prior)

        size = q.shape[0] // 2
        low, high = slice(0, size), slice(size, 2 * size)
        first = scores(low)
        second = scores(high)
        reduce(low, first)
        reduce(high, second)

    for (start, count), pair_ref in zip(groups, pairs):
        pl.when((at >= start) & (at < start + count))(functools.partial(work, pair_ref))

    @pl.when(at == heads)
    def _():
        send_ref[0] = send_logs(log_ref[...])


def text_partial(scal, valid, query_text, mine, pairs, groups, key_text, value_text):
    _, heads, time_tiles, _, _, _ = mine.shape
    text = query_text.shape[0]
    block = (2, 1, time_tiles, 2, VOL, HD)

    def of_group(start, count):
        return pl.BlockSpec(block, lambda i, s: (0, jnp.clip(i - start, 0, count - 1), 0, 0, 0, 0))

    word = pl.BlockSpec((text, HD), lambda i, s: (0, s[4] * heads + jnp.minimum(i, heads - 1)))
    return pl.pallas_call(
        functools.partial(text_body, groups),
        grid_spec=pltpu.PrefetchScalarGridSpec(
            num_scalar_prefetch=1,
            grid=(heads + 1,),
            in_specs=[pl.BlockSpec((1, text), lambda i, s: (0, 0)), word, of_group(0, heads), word, word]
            + [of_group(start, count) for start, count in groups],
            out_specs=[
                pl.BlockSpec((1, text, HD), lambda i, s: (jnp.minimum(i, heads - 1), 0, 0)),
                pl.BlockSpec((text, HD), lambda i, s: (0, 0)),
                pl.BlockSpec((1, text, HD), lambda i, s: (i, 0, 0)),
            ],
        ),
        out_shape=[
            jax.ShapeDtypeStruct((heads, text, HD), F32),
            jax.ShapeDtypeStruct((text, HD), F32),
            jax.ShapeDtypeStruct((heads + 1, text, HD), BF16),
        ],
        compiler_params=pltpu.CompilerParams(vmem_limit_bytes=VMEM),
        cost_estimate=cost(0),
        name="text",
    )(scal, valid, query_text, mine, key_text, value_text, *pairs)


def combine(parts, heads):
    logs = [part[1] for part in parts]
    top = functools.reduce(jnp.maximum, logs)
    weights = [jnp.exp(log - top) for log in logs]
    total = functools.reduce(jnp.add, weights)
    weights = [weight / total for weight in weights]
    outs = []
    for head in range(heads):
        terms = [weight[:, head : head + 1] * part[0](head) for weight, part in zip(weights, parts)]
        outs.append(functools.reduce(jnp.add, terms))
    return outs, top + jnp.log(total)


def join_body(sum_ref, log_ref, got_ref, out_ref):
    heads = sum_ref.shape[0]
    own = (lambda head: sum_ref[head], log_ref[...])
    got = (lambda head: got_ref[head].astype(F32), read_logs(got_ref[heads]))
    outs, logs = combine([own, got], heads)
    for head in range(heads):
        out_ref[head] = outs[head].astype(BF16)
    out_ref[heads] = send_logs(logs)


def join(sums, logs, got):
    return pl.pallas_call(
        join_body,
        out_shape=jax.ShapeDtypeStruct(got.shape, BF16),
        compiler_params=pltpu.CompilerParams(vmem_limit_bytes=VMEM),
        cost_estimate=cost(0),
        name="join",
    )(sums, logs, got)


def finish_body(scal, own_ref, got_ref, out_ref):
    heads = own_ref.shape[0] - 1
    low = scal[5] > 0
    parts = []
    for flag in (low, jnp.logical_not(low)):

        def pick(index, flag=flag):
            return jnp.where(flag, own_ref[index].astype(F32), got_ref[index].astype(F32))

        parts.append((pick, read_logs(pick(heads))))
    outs, _ = combine(parts, heads)
    for head in range(heads):
        out_ref[:, head * HD : (head + 1) * HD] = outs[head].astype(BF16)


def finish(scal, own, got):
    heads, text, _ = own.shape
    return pl.pallas_call(
        finish_body,
        grid_spec=pltpu.PrefetchScalarGridSpec(
            num_scalar_prefetch=1,
            grid=(1,),
            in_specs=[pl.BlockSpec(own.shape, lambda i, s: (0, 0, 0))] * 2,
            out_specs=pl.BlockSpec((text, (heads - 1) * HD), lambda i, s: (0, 0)),
        ),
        out_shape=jax.ShapeDtypeStruct((text, (heads - 1) * HD), BF16),
        compiler_params=pltpu.CompilerParams(vmem_limit_bytes=VMEM),
        cost_estimate=cost(0),
        name="finish",
    )(scal, own, got)


def after(value, *others):
    return lax.optimization_barrier((value, *others))[0]


def shards(query_video, key_video, value_video, query_text, key_text, value_text, text_valid):
    features = query_video.shape[3]
    heads = features // HD
    strips = lax.axis_size("tm")
    strip = lax.axis_index("tm")
    half = lax.axis_index("height")
    half_heads = heads // 2

    def swap(array):
        return lax.ppermute(array, "height", [(0, 1), (1, 0)])

    up = [(i, i + 1) for i in range(strips - 1)]
    down = [(i + 1, i) for i in range(strips - 1)]
    scal = jnp.stack(
        [1 - half, strip > 0, strip < strips - 1, strip == 0, half, strip < strips // 2]
    ).astype(jnp.int32)
    valid = text_valid.reshape(1, -1)
    groups = head_groups(half_heads)

    def to_neighbours(array):
        return lax.ppermute(array, "tm", up), lax.ppermute(array, "tm", down)

    (mine,) = pack_half(scal, key_video, value_video, (half_heads,))
    mine_sides = to_neighbours(mine)
    theirs = pack_half(after(scal, mine), key_video, value_video, [count for _, count in groups], query_video)
    pairs = [swap(array) for array in theirs[:-1]]
    pair_query = swap(theirs[-1])
    sums, logs, sent = text_partial(after(scal, pair_query), valid, query_text, mine, pairs, groups, key_text, value_text)

    middle = strips // 2
    for step in range(1, middle):
        got = lax.ppermute(sent, "tm", [(step - 1, step), (strips - step, strips - step - 1)])
        sent = join(sums, after(logs, *mine_sides), got)
    got = lax.ppermute(sent, "tm", [(middle - 1, middle), (middle, middle - 1)])

    def place(whole, part, start):
        column = ((1 - half) * half_heads + start) * HD
        return lax.dynamic_update_slice_in_dim(whole, part, column, 3)

    out_video = None
    waiting = []
    for index, (start, count) in enumerate(groups):
        pair = (pairs[index], *to_neighbours(pairs[index]))
        out_video, given = video_group(
            scal, valid, query_video, pair_query, (mine, *mine_sides), pair, key_text, value_text, out_video, start, count
        )
        if index == 0:
            opened = after(scal, out_video)
        for part in waiting:
            out_video = place(out_video, *part)
        waiting = [(swap(given), start)]
    for part in waiting:
        out_video = place(out_video, *part)

    done = finish(opened, sent, got)
    for step in range(middle - 1, 0, -1):
        got = lax.ppermute(done, "tm", [(step, step - 1), (strips - step - 1, strips - step)])
        done = jnp.where((strip == step - 1) | (strip == strips - step), got, done)
    other = swap(done)
    first = half == 0
    out_text = jnp.concatenate([jnp.where(first, done, other), jnp.where(first, other, done)], axis=1)
    return (out_video, out_text)


def solution(mesh):
    if mesh.shape["height"] != 2 or mesh.shape["tm"] % 2:
        raise ValueError("unsupported mesh")
    placed = (
        P("grp", "height", "tm", "head"),
        P("grp", "height", "tm", "head"),
        P("grp", "height", "tm", "head"),
        P("grp", "head"),
        P("grp", "head"),
        P("grp", "head"),
        P("grp"),
    )
    return jax.shard_map(
        shards,
        mesh=mesh,
        in_specs=placed,
        out_specs=(P("grp", "height", "tm", "head"), P("grp", "head")),
        check_vma=False,
    )
```

```python
import functools
import math

import jax
import jax.numpy as jnp
from jax import lax
from jax.experimental import pallas as pl
from jax.experimental.pallas import tpu as pltpu
from jax.sharding import PartitionSpec as P

HD = 128
TILE = 4
VOL = TILE**3
BF16 = jnp.bfloat16
F32 = jnp.float32
SCALE = 1.0 / math.sqrt(HD)
SCALE_2 = SCALE * math.log2(math.e)
VMEM = 255 << 18
THIRD = 32
SIZES = (3, 3)


def cost(microseconds):
    return pl.CostEstimate(flops=int(microseconds * 1.15e9), bytes_accessed=1, transcendentals=0)


def head_groups(heads):
    sizes = SIZES if heads == sum(SIZES) else [heads - 1, 1]
    starts = [sum(sizes[:i]) for i in range(len(sizes))]
    return list(zip(starts, sizes))


def dot_nt(a, b):
    return lax.dot_general(a, b, (((1,), (1,)), ((), ())), preferred_element_type=F32)


def dot_nn(a, b):
    return lax.dot_general(a, b, (((1,), (0,)), ((), ())), preferred_element_type=F32)


def weigh(p, v):
    return dot_nn(p.astype(BF16), jnp.concatenate([v, jnp.ones_like(v)], axis=1))


def pack_body(sizes, scal, *rest):
    k_ref, v_ref = rest[:2]
    tiles = rest[-len(sizes) - 1 : -1] if len(rest) == len(sizes) + 4 else rest[-len(sizes) :]
    head = 0
    for size, kv_ref in zip(sizes, tiles):
        for at in range(size):
            lanes = slice(head * HD, (head + 1) * HD)
            head += 1
            for which, ref in enumerate((k_ref, v_ref)):
                for t in range(ref.shape[0] // TILE):
                    frames = slice(t * TILE, (t + 1) * TILE)
                    for r in range(ref.shape[1] // TILE):
                        tile = ref[frames, r * TILE : (r + 1) * TILE, :, lanes]
                        kv_ref[which, at, t, r] = tile.reshape(VOL, HD)
    if len(rest) == len(sizes) + 4:
        rest[-1][...] = rest[2][...]


def pack_half(scal, key_video, value_video, sizes, query_video=None):
    frames, rows, cols, features = key_video.shape
    time_tiles = frames // TILE
    row_tiles = rows // TILE
    theirs = query_video is not None
    depth = 2 if time_tiles % 2 == 0 else 1
    block = pl.BlockSpec(
        (depth * TILE, rows, cols, features // 2), lambda t, s: (t, 0, 0, 1 - s[4] if theirs else s[4])
    )
    operands = [key_video, value_video]
    out_specs = [
        pl.BlockSpec((2, size, depth, row_tiles, VOL, HD), lambda t, s: (0, 0, t, 0, 0, 0)) for size in sizes
    ]
    out_shape = [jax.ShapeDtypeStruct((2, size, time_tiles, row_tiles, VOL, HD), BF16) for size in sizes]
    if theirs:
        operands.append(query_video)
        out_specs.append(pl.BlockSpec((depth * TILE, rows, cols, features // 2), lambda t, s: (t, 0, 0, 0)))
        out_shape.append(jax.ShapeDtypeStruct((frames, rows, cols, features // 2), BF16))
    return pl.pallas_call(
        functools.partial(pack_body, sizes),
        grid_spec=pltpu.PrefetchScalarGridSpec(
            num_scalar_prefetch=1, grid=(time_tiles // depth,), in_specs=[block] * len(operands), out_specs=out_specs
        ),
        out_shape=out_shape,
        compiler_params=pltpu.CompilerParams(vmem_limit_bytes=VMEM),
        cost_estimate=cost(0),
        name="pack",
    )(scal, *operands)


def video_body(scal, valid_ref, own_q, pair_q, *rest):
    own_tiles, pair_tiles, (tk_ref, tv_ref) = rest[:3], rest[3:6], rest[6:8]
    own_out, pair_out = rest[-2:]
    has_left = scal[1] > 0
    has_right = scal[2] > 0
    time_tiles = own_q.shape[0] // TILE
    open_keys = valid_ref[...] > 0

    def load(ref, which, first, last, row):
        picked = ref[which, 0, first:last] if row is None else ref[which, 0, first:last, pl.ds(row, 1)]
        return picked.reshape(picked.shape[0] * picked.shape[1] * VOL, HD)

    def scores(step):
        part, t = step
        q_ref = (own_q, pair_q)[part]
        near = scal[0] if part == 0 else 1 - scal[0]
        far_rows = pl.ds((1 - near) * TILE, TILE)
        near_rows = pl.ds(near * TILE, TILE)
        own, left, right = (own_tiles, pair_tiles)[part]
        edge, edge_left, edge_right = (pair_tiles, own_tiles)[part]
        row = 1 - near
        first = max(t - 1, 0)
        last = min(t + 1, time_tiles - 1) + 1
        frames = slice(t * TILE, (t + 1) * TILE)
        q_far = q_ref[frames, far_rows, :, :].reshape(VOL, HD)
        q_near = q_ref[frames, near_rows, :, :].reshape(VOL, HD)
        q_all = jnp.concatenate([q_far, q_near], axis=0)
        s_text = jnp.where(open_keys, dot_nt(q_all, tk_ref[...]), -jnp.inf)
        wide = [(s_text, None, None)]
        for ref, ok in ((own, None), (left, has_left), (right, has_right)):
            wide.append((dot_nt(q_all, load(ref, 0, first, last, None)), ref, ok))
        thin = []
        for ref, ok in ((edge, None), (edge_left, has_left), (edge_right, has_right)):
            thin.append((dot_nt(q_near, load(ref, 0, first, last, row)), ref, ok))
        return first, last, wide, thin, row, far_rows, near_rows

    def peak(entries):
        tops = []
        for s, _, ok in entries:
            top = jnp.max(s, axis=1, keepdims=True)
            tops.append(top if ok is None else jnp.where(ok, top, -jnp.inf))
        return functools.reduce(jnp.maximum, tops)

    def gather(entries, m, first, last, row):
        summed = None
        for s, ref, ok in entries:
            base = m if ok is None else jnp.where(ok, m, jnp.inf)
            v = tv_ref[...] if ref is None else load(ref, 1, first, last, row)
            part = weigh(jnp.exp2((s - base) * SCALE_2), v)
            summed = part if summed is None else summed + part
        return summed

    def finish(step, state):
        part, t = step
        out_ref = (own_out, pair_out)[part]
        first, last, wide, thin, row, far_rows, near_rows = state
        frames = slice(t * TILE, (t + 1) * TILE)
        m_all = peak(wide)
        m_near = jnp.maximum(m_all[VOL:], peak(thin))
        m_all = jnp.concatenate([m_all[:VOL], m_near], axis=0)
        summed = gather(wide, m_all, first, last, None)
        far = summed[:VOL]
        close = summed[VOL:] + gather(thin, m_near, first, last, row)
        for rows, value in ((far_rows, far), (near_rows, close)):
            out = value[:, :HD] / value[:, HD:]
            out_ref[frames, rows, :, :] = out.astype(BF16).reshape(TILE, TILE, TILE, HD)

    steps = [(part, t) for part in range(2) for t in range(time_tiles)]
    state = scores(steps[0])
    for at, step in enumerate(steps):
        following = scores(steps[at + 1]) if at + 1 < len(steps) else None
        finish(step, state)
        state = following


def video_group(scal, valid, query_video, pair_query, mine, pair, key_text, value_text, prior, start, count):
    frames, rows, cols, _ = query_video.shape
    half_heads = pair_query.shape[3] // HD
    time_tiles = frames // TILE
    text = key_text.shape[0]
    block = (frames, rows, cols, HD)
    own_head = pl.BlockSpec(block, lambda i, s: (0, 0, 0, s[4] * half_heads + start + i))
    pair_head = pl.BlockSpec(block, lambda i, s: (0, 0, 0, start + i))
    of_half = pl.BlockSpec((2, 1, time_tiles, 2, VOL, HD), lambda i, s: (0, start + i, 0, 0, 0, 0))
    of_group = pl.BlockSpec((2, 1, time_tiles, 2, VOL, HD), lambda i, s: (0, i, 0, 0, 0, 0))
    word = pl.BlockSpec((text, HD), lambda i, s: (0, s[4] * half_heads + start + i))
    specs = [pl.BlockSpec((1, text), lambda i, s: (0, 0)), own_head, pair_head]
    specs += [of_half] * 3 + [of_group] * 3 + [word, word]
    operands = [scal, valid, query_video, pair_query, *mine, *pair, key_text, value_text]
    aliases = {}
    for at, array in enumerate(prior):
        specs.append(pl.BlockSpec(memory_space=pl.ANY))
        aliases[len(operands)] = at
        operands.append(array)
    return pl.pallas_call(
        video_body,
        grid_spec=pltpu.PrefetchScalarGridSpec(
            num_scalar_prefetch=1,
            grid=(count,),
            in_specs=specs,
            out_specs=[own_head, pair_head],
        ),
        out_shape=[
            jax.ShapeDtypeStruct(query_video.shape, BF16),
            jax.ShapeDtypeStruct(pair_query.shape, BF16),
        ],
        input_output_aliases=aliases,
        compiler_params=pltpu.CompilerParams(vmem_limit_bytes=VMEM),
        cost_estimate=cost(0),
        name="video",
    )(*operands)


def lane_of(shape):
    return lax.broadcasted_iota(jnp.int32, shape, len(shape) - 1)


def send_logs(logs):
    high = logs.astype(BF16).astype(F32)
    mid = (logs - high).astype(BF16).astype(F32)
    low = logs - high - mid
    lane = lane_of(logs.shape)
    whole = jnp.where(lane < THIRD, high, 0.0)
    whole = jnp.where((lane >= THIRD) & (lane < 2 * THIRD), pltpu.roll(mid, THIRD, 1), whole)
    whole = jnp.where((lane >= 2 * THIRD) & (lane < 3 * THIRD), pltpu.roll(low, 2 * THIRD, 1), whole)
    return jnp.where(lane == HD - 1, 1.0, whole).astype(BF16)


def read_logs(sent):
    whole = sent.astype(F32)
    logs = whole + pltpu.roll(whole, HD - THIRD, 1) + pltpu.roll(whole, HD - 2 * THIRD, 1)
    return jnp.where(whole[:, HD - 1 :] > 0, logs, -jnp.inf)


def text_body(groups, scal, valid_ref, q_ref, mine_ref, tk_ref, tv_ref, *rest):
    pairs = rest[: len(groups)]
    sum_ref, log_ref, send_ref = rest[len(groups) :]
    at = pl.program_id(0)
    heads = pl.num_programs(0) - 1

    def work(pair_ref):
        q = q_ref[...]

        def tokens(ref, which):
            whole = ref[which, 0]
            return whole.reshape(whole.shape[0] * whole.shape[1] * VOL, HD)

        def scores(rows):
            near = jnp.where((valid_ref[...] > 0) & (scal[3] > 0), dot_nt(q[rows], tk_ref[...]), -jnp.inf)
            return [dot_nt(q[rows], tokens(mine_ref, 0)), dot_nt(q[rows], tokens(pair_ref, 0)), near]

        def reduce(rows, parts):
            m = functools.reduce(jnp.maximum, [jnp.max(s, axis=1, keepdims=True) for s in parts])
            values = (tokens(mine_ref, 1), tokens(pair_ref, 1), tv_ref[...])
            both = functools.reduce(
                jnp.add, [weigh(jnp.exp2((s - m) * SCALE_2), v) for s, v in zip(parts, values)]
            )
            total = both[:, HD:]
            out = both[:, :HD] / total
            sum_ref[0, rows] = out
            send_ref[0, rows] = out.astype(BF16)
            logs = m * SCALE + jnp.log(total)
            prior = jnp.where(at == 0, 0.0, log_ref[rows])
            log_ref[rows] = jnp.where(lane_of(logs.shape) == at, logs, prior)

        size = q.shape[0] // 2
        low, high = slice(0, size), slice(size, 2 * size)
        first = scores(low)
        second = scores(high)
        reduce(low, first)
        reduce(high, second)

    for (start, count), pair_ref in zip(groups, pairs):
        pl.when((at >= start) & (at < start + count))(functools.partial(work, pair_ref))

    @pl.when(at == heads)
    def _():
        send_ref[0] = send_logs(log_ref[...])


def text_partial(scal, valid, query_text, mine, pairs, groups, key_text, value_text):
    _, heads, time_tiles, _, _, _ = mine.shape
    text = query_text.shape[0]
    block = (2, 1, time_tiles, 2, VOL, HD)

    def of_group(start, count):
        return pl.BlockSpec(block, lambda i, s: (0, jnp.clip(i - start, 0, count - 1), 0, 0, 0, 0))

    word = pl.BlockSpec((text, HD), lambda i, s: (0, s[4] * heads + jnp.minimum(i, heads - 1)))
    return pl.pallas_call(
        functools.partial(text_body, groups),
        grid_spec=pltpu.PrefetchScalarGridSpec(
            num_scalar_prefetch=1,
            grid=(heads + 1,),
            in_specs=[pl.BlockSpec((1, text), lambda i, s: (0, 0)), word, of_group(0, heads), word, word]
            + [of_group(start, count) for start, count in groups],
            out_specs=[
                pl.BlockSpec((1, text, HD), lambda i, s: (jnp.minimum(i, heads - 1), 0, 0)),
                pl.BlockSpec((text, HD), lambda i, s: (0, 0)),
                pl.BlockSpec((1, text, HD), lambda i, s: (i, 0, 0)),
            ],
        ),
        out_shape=[
            jax.ShapeDtypeStruct((heads, text, HD), F32),
            jax.ShapeDtypeStruct((text, HD), F32),
            jax.ShapeDtypeStruct((heads + 1, text, HD), BF16),
        ],
        compiler_params=pltpu.CompilerParams(vmem_limit_bytes=VMEM),
        cost_estimate=cost(0),
        name="text",
    )(scal, valid, query_text, mine, key_text, value_text, *pairs)


def combine(parts, heads):
    logs = [part[1] for part in parts]
    top = functools.reduce(jnp.maximum, logs)
    weights = [jnp.exp(log - top) for log in logs]
    total = functools.reduce(jnp.add, weights)
    weights = [weight / total for weight in weights]
    outs = []
    for head in range(heads):
        terms = [weight[:, head : head + 1] * part[0](head) for weight, part in zip(weights, parts)]
        outs.append(functools.reduce(jnp.add, terms))
    return outs, top + jnp.log(total)


def join_body(sum_ref, log_ref, got_ref, out_ref):
    heads = sum_ref.shape[0]
    own = (lambda head: sum_ref[head], log_ref[...])
    got = (lambda head: got_ref[head].astype(F32), read_logs(got_ref[heads]))
    outs, logs = combine([own, got], heads)
    for head in range(heads):
        out_ref[head] = outs[head].astype(BF16)
    out_ref[heads] = send_logs(logs)


def join(sums, logs, got):
    return pl.pallas_call(
        join_body,
        out_shape=jax.ShapeDtypeStruct(got.shape, BF16),
        compiler_params=pltpu.CompilerParams(vmem_limit_bytes=VMEM),
        cost_estimate=cost(0),
        name="join",
    )(sums, logs, got)


def finish_body(scal, own_ref, got_ref, out_ref):
    heads = own_ref.shape[0] - 1
    low = scal[5] > 0
    parts = []
    for flag in (low, jnp.logical_not(low)):

        def pick(index, flag=flag):
            return jnp.where(flag, own_ref[index].astype(F32), got_ref[index].astype(F32))

        parts.append((pick, read_logs(pick(heads))))
    outs, _ = combine(parts, heads)
    for head in range(heads):
        out_ref[:, head * HD : (head + 1) * HD] = outs[head].astype(BF16)


def finish(scal, own, got):
    heads, text, _ = own.shape
    return pl.pallas_call(
        finish_body,
        grid_spec=pltpu.PrefetchScalarGridSpec(
            num_scalar_prefetch=1,
            grid=(1,),
            in_specs=[pl.BlockSpec(own.shape, lambda i, s: (0, 0, 0))] * 2,
            out_specs=pl.BlockSpec((text, (heads - 1) * HD), lambda i, s: (0, 0)),
        ),
        out_shape=jax.ShapeDtypeStruct((text, (heads - 1) * HD), BF16),
        compiler_params=pltpu.CompilerParams(vmem_limit_bytes=VMEM),
        cost_estimate=cost(0),
        name="finish",
    )(scal, own, got)


def after(value, *others):
    return lax.optimization_barrier((value, *others))[0]


def shards(query_video, key_video, value_video, query_text, key_text, value_text, text_valid):
    features = query_video.shape[3]
    heads = features // HD
    strips = lax.axis_size("tm")
    strip = lax.axis_index("tm")
    half = lax.axis_index("height")
    half_heads = heads // 2

    def swap(array):
        return lax.ppermute(array, "height", [(0, 1), (1, 0)])

    up = [(i, i + 1) for i in range(strips - 1)]
    down = [(i + 1, i) for i in range(strips - 1)]
    scal = jnp.stack(
        [1 - half, strip > 0, strip < strips - 1, strip == 0, half, strip < strips // 2]
    ).astype(jnp.int32)
    valid = text_valid.reshape(1, -1)
    groups = head_groups(half_heads)

    def to_neighbours(array):
        return lax.ppermute(array, "tm", up), lax.ppermute(array, "tm", down)

    (mine,) = pack_half(scal, key_video, value_video, (half_heads,))
    mine_sides = to_neighbours(mine)
    theirs = pack_half(after(scal, mine), key_video, value_video, [count for _, count in groups], query_video)
    pairs = [swap(array) for array in theirs[:-1]]
    pair_query = swap(theirs[-1])
    sums, logs, sent = text_partial(after(scal, pair_query), valid, query_text, mine, pairs, groups, key_text, value_text)

    middle = strips // 2
    for step in range(1, middle):
        got = lax.ppermute(sent, "tm", [(step - 1, step), (strips - step, strips - step - 1)])
        sent = join(sums, after(logs, *mine_sides), got)
    got = lax.ppermute(sent, "tm", [(middle - 1, middle), (middle, middle - 1)])

    outs = ()
    for index, (start, count) in enumerate(groups):
        pair = (pairs[index], *to_neighbours(after(pairs[index], sent) if index else pairs[index]))
        outs = video_group(
            scal, valid, query_video, pair_query, (mine, *mine_sides), pair, key_text, value_text, outs, start, count
        )
        if index == 0:
            opened = after(scal, outs[0])
    column = (1 - half) * half_heads * HD
    out_video = lax.dynamic_update_slice_in_dim(outs[0], swap(outs[1]), column, 3)

    done = finish(opened, sent, got)
    for step in range(middle - 1, 0, -1):
        got = lax.ppermute(done, "tm", [(step, step - 1), (strips - step - 1, strips - step)])
        done = jnp.where((strip == step - 1) | (strip == strips - step), after(got, outs[1]), done)
    other = swap(done)
    first = half == 0
    out_text = jnp.concatenate([jnp.where(first, done, other), jnp.where(first, other, done)], axis=1)
    return (out_video, out_text)


def solution(mesh):
    if mesh.shape["height"] != 2 or mesh.shape["tm"] % 2:
        raise ValueError("unsupported mesh")
    placed = (
        P("grp", "height", "tm", "head"),
        P("grp", "height", "tm", "head"),
        P("grp", "height", "tm", "head"),
        P("grp", "head"),
        P("grp", "head"),
        P("grp", "head"),
        P("grp"),
    )
    return jax.shard_map(
        shards,
        mesh=mesh,
        in_specs=placed,
        out_specs=(P("grp", "height", "tm", "head"), P("grp", "head")),
        check_vma=False,
    )
```

```python
import functools
import math

import jax
import jax.numpy as jnp
from jax import lax
from jax.experimental import pallas as pl
from jax.experimental.pallas import tpu as pltpu
from jax.sharding import PartitionSpec as P

HD = 128
TILE = 4
VOL = TILE**3
BF16 = jnp.bfloat16
F32 = jnp.float32
SCALE = 1.0 / math.sqrt(HD)
SCALE_2 = SCALE * math.log2(math.e)
VMEM = 255 << 18
THIRD = 32
SIZES = (3, 3)


def cost(microseconds):
    return pl.CostEstimate(flops=int(microseconds * 1.15e9), bytes_accessed=1, transcendentals=0)


def head_groups(heads):
    sizes = SIZES if heads == sum(SIZES) else [heads - 1, 1]
    starts = [sum(sizes[:i]) for i in range(len(sizes))]
    return list(zip(starts, sizes))


def dot_nt(a, b):
    return lax.dot_general(a, b, (((1,), (1,)), ((), ())), preferred_element_type=F32)


def dot_nn(a, b):
    return lax.dot_general(a, b, (((1,), (0,)), ((), ())), preferred_element_type=F32)


def weigh(p, v):
    return dot_nn(p.astype(BF16), jnp.concatenate([v, jnp.ones_like(v)], axis=1))


def pack_body(sizes, scal, *rest):
    k_ref, v_ref = rest[:2]
    tiles = rest[-len(sizes) - 1 : -1] if len(rest) == len(sizes) + 4 else rest[-len(sizes) :]
    head = 0
    for size, kv_ref in zip(sizes, tiles):
        for at in range(size):
            lanes = slice(head * HD, (head + 1) * HD)
            head += 1
            for which, ref in enumerate((k_ref, v_ref)):
                for t in range(ref.shape[0] // TILE):
                    frames = slice(t * TILE, (t + 1) * TILE)
                    for r in range(ref.shape[1] // TILE):
                        tile = ref[frames, r * TILE : (r + 1) * TILE, :, lanes]
                        kv_ref[which, at, t, r] = tile.reshape(VOL, HD)
    if len(rest) == len(sizes) + 4:
        rest[-1][...] = rest[2][...]


def pack_half(scal, key_video, value_video, sizes, query_video=None):
    frames, rows, cols, features = key_video.shape
    time_tiles = frames // TILE
    row_tiles = rows // TILE
    theirs = query_video is not None
    depth = 2 if time_tiles % 2 == 0 else 1
    block = pl.BlockSpec(
        (depth * TILE, rows, cols, features // 2), lambda t, s: (t, 0, 0, 1 - s[4] if theirs else s[4])
    )
    operands = [key_video, value_video]
    out_specs = [
        pl.BlockSpec((2, size, depth, row_tiles, VOL, HD), lambda t, s: (0, 0, t, 0, 0, 0)) for size in sizes
    ]
    out_shape = [jax.ShapeDtypeStruct((2, size, time_tiles, row_tiles, VOL, HD), BF16) for size in sizes]
    if theirs:
        operands.append(query_video)
        out_specs.append(pl.BlockSpec((depth * TILE, rows, cols, features // 2), lambda t, s: (t, 0, 0, 0)))
        out_shape.append(jax.ShapeDtypeStruct((frames, rows, cols, features // 2), BF16))
    return pl.pallas_call(
        functools.partial(pack_body, sizes),
        grid_spec=pltpu.PrefetchScalarGridSpec(
            num_scalar_prefetch=1, grid=(time_tiles // depth,), in_specs=[block] * len(operands), out_specs=out_specs
        ),
        out_shape=out_shape,
        compiler_params=pltpu.CompilerParams(vmem_limit_bytes=VMEM),
        cost_estimate=cost(0),
        name="pack",
    )(scal, *operands)


def video_body(scal, valid_ref, own_q, pair_q, *rest):
    own_tiles, pair_tiles, (tk_ref, tv_ref) = rest[:3], rest[3:6], rest[6:8]
    own_out, pair_out = rest[-2:]
    has_left = scal[1] > 0
    has_right = scal[2] > 0
    time_tiles = own_q.shape[0] // TILE
    open_keys = valid_ref[...] > 0

    def load(ref, which, first, last, row):
        picked = ref[which, 0, first:last] if row is None else ref[which, 0, first:last, pl.ds(row, 1)]
        return picked.reshape(picked.shape[0] * picked.shape[1] * VOL, HD)

    def scores(step):
        part, t = step
        q_ref = (own_q, pair_q)[part]
        near = scal[0] if part == 0 else 1 - scal[0]
        far_rows = pl.ds((1 - near) * TILE, TILE)
        near_rows = pl.ds(near * TILE, TILE)
        own, left, right = (own_tiles, pair_tiles)[part]
        edge, edge_left, edge_right = (pair_tiles, own_tiles)[part]
        row = 1 - near
        first = max(t - 1, 0)
        last = min(t + 1, time_tiles - 1) + 1
        frames = slice(t * TILE, (t + 1) * TILE)
        q_far = q_ref[frames, far_rows, :, :].reshape(VOL, HD)
        q_near = q_ref[frames, near_rows, :, :].reshape(VOL, HD)
        q_all = jnp.concatenate([q_far, q_near], axis=0)
        s_text = jnp.where(open_keys, dot_nt(q_all, tk_ref[...]), -jnp.inf)
        wide = [(s_text, None, None)]
        for ref, ok in ((own, None), (left, has_left), (right, has_right)):
            wide.append((dot_nt(q_all, load(ref, 0, first, last, None)), ref, ok))
        thin = []
        for ref, ok in ((edge, None), (edge_left, has_left), (edge_right, has_right)):
            thin.append((dot_nt(q_near, load(ref, 0, first, last, row)), ref, ok))
        return first, last, wide, thin, row, far_rows, near_rows

    def peak(entries):
        tops = {}
        for s, _, ok in entries:
            local = {}
            for at in range(0, s.shape[1], HD):
                piece = s[:, at : at + HD]
                width = piece.shape[1]
                local[width] = jnp.maximum(local[width], piece) if width in local else piece
            for width, top in local.items():
                top = top if ok is None else jnp.where(ok, top, -jnp.inf)
                tops[width] = jnp.maximum(tops[width], top) if width in tops else top
        return functools.reduce(jnp.maximum, [jnp.max(top, axis=1, keepdims=True) for top in tops.values()])

    def gather(entries, m, first, last, row):
        summed = None
        for s, ref, ok in entries:
            base = m if ok is None else jnp.where(ok, m, jnp.inf)
            v = tv_ref[...] if ref is None else load(ref, 1, first, last, row)
            part = weigh(jnp.exp2((s - base) * SCALE_2), v)
            summed = part if summed is None else summed + part
        return summed

    def finish(step, state):
        part, t = step
        out_ref = (own_out, pair_out)[part]
        first, last, wide, thin, row, far_rows, near_rows = state
        frames = slice(t * TILE, (t + 1) * TILE)
        m_all = peak(wide)
        m_near = jnp.maximum(m_all[VOL:], peak(thin))
        m_all = jnp.concatenate([m_all[:VOL], m_near], axis=0)
        summed = gather(wide, m_all, first, last, None)
        far = summed[:VOL]
        close = summed[VOL:] + gather(thin, m_near, first, last, row)
        for rows, value in ((far_rows, far), (near_rows, close)):
            out = value[:, :HD] / value[:, HD:]
            out_ref[frames, rows, :, :] = out.astype(BF16).reshape(TILE, TILE, TILE, HD)

    steps = [(part, t) for part in range(2) for t in range(time_tiles)]
    state = scores(steps[0])
    for at, step in enumerate(steps):
        following = scores(steps[at + 1]) if at + 1 < len(steps) else None
        finish(step, state)
        state = following


def video_group(scal, valid, query_video, pair_query, mine, pair, key_text, value_text, prior, start, count):
    frames, rows, cols, _ = query_video.shape
    half_heads = pair_query.shape[3] // HD
    time_tiles = frames // TILE
    text = key_text.shape[0]
    block = (frames, rows, cols, HD)
    own_head = pl.BlockSpec(block, lambda i, s: (0, 0, 0, s[4] * half_heads + start + i))
    pair_head = pl.BlockSpec(block, lambda i, s: (0, 0, 0, start + i))
    of_half = pl.BlockSpec((2, 1, time_tiles, 2, VOL, HD), lambda i, s: (0, start + i, 0, 0, 0, 0))
    of_group = pl.BlockSpec((2, 1, time_tiles, 2, VOL, HD), lambda i, s: (0, i, 0, 0, 0, 0))
    word = pl.BlockSpec((text, HD), lambda i, s: (0, s[4] * half_heads + start + i))
    specs = [pl.BlockSpec((1, text), lambda i, s: (0, 0)), own_head, pair_head]
    specs += [of_half] * 3 + [of_group] * 3 + [word, word]
    operands = [scal, valid, query_video, pair_query, *mine, *pair, key_text, value_text]
    aliases = {}
    for at, array in enumerate(prior):
        specs.append(pl.BlockSpec(memory_space=pl.ANY))
        aliases[len(operands)] = at
        operands.append(array)
    return pl.pallas_call(
        video_body,
        grid_spec=pltpu.PrefetchScalarGridSpec(
            num_scalar_prefetch=1,
            grid=(count,),
            in_specs=specs,
            out_specs=[own_head, pair_head],
        ),
        out_shape=[
            jax.ShapeDtypeStruct(query_video.shape, BF16),
            jax.ShapeDtypeStruct(pair_query.shape, BF16),
        ],
        input_output_aliases=aliases,
        compiler_params=pltpu.CompilerParams(vmem_limit_bytes=VMEM),
        cost_estimate=cost(0),
        name="video",
    )(*operands)


def lane_of(shape):
    return lax.broadcasted_iota(jnp.int32, shape, len(shape) - 1)


def send_logs(logs):
    high = logs.astype(BF16).astype(F32)
    mid = (logs - high).astype(BF16).astype(F32)
    low = logs - high - mid
    lane = lane_of(logs.shape)
    whole = jnp.where(lane < THIRD, high, 0.0)
    whole = jnp.where((lane >= THIRD) & (lane < 2 * THIRD), pltpu.roll(mid, THIRD, 1), whole)
    whole = jnp.where((lane >= 2 * THIRD) & (lane < 3 * THIRD), pltpu.roll(low, 2 * THIRD, 1), whole)
    return jnp.where(lane == HD - 1, 1.0, whole).astype(BF16)


def read_logs(sent):
    whole = sent.astype(F32)
    logs = whole + pltpu.roll(whole, HD - THIRD, 1) + pltpu.roll(whole, HD - 2 * THIRD, 1)
    return jnp.where(whole[:, HD - 1 :] > 0, logs, -jnp.inf)


def text_body(groups, scal, valid_ref, q_ref, mine_ref, tk_ref, tv_ref, *rest):
    pairs = rest[: len(groups)]
    sum_ref, log_ref, send_ref = rest[len(groups) :]
    at = pl.program_id(0)
    heads = pl.num_programs(0) - 1

    def work(pair_ref):
        q = q_ref[...]

        def tokens(ref, which):
            whole = ref[which, 0]
            return whole.reshape(whole.shape[0] * whole.shape[1] * VOL, HD)

        def scores(rows):
            near = jnp.where((valid_ref[...] > 0) & (scal[3] > 0), dot_nt(q[rows], tk_ref[...]), -jnp.inf)
            return [dot_nt(q[rows], tokens(mine_ref, 0)), dot_nt(q[rows], tokens(pair_ref, 0)), near]

        def reduce(rows, parts):
            m = functools.reduce(jnp.maximum, [jnp.max(s, axis=1, keepdims=True) for s in parts])
            values = (tokens(mine_ref, 1), tokens(pair_ref, 1), tv_ref[...])
            both = functools.reduce(
                jnp.add, [weigh(jnp.exp2((s - m) * SCALE_2), v) for s, v in zip(parts, values)]
            )
            total = both[:, HD:]
            out = both[:, :HD] / total
            sum_ref[0, rows] = out
            send_ref[0, rows] = out.astype(BF16)
            logs = m * SCALE + jnp.log(total)
            prior = jnp.where(at == 0, 0.0, log_ref[rows])
            log_ref[rows] = jnp.where(lane_of(logs.shape) == at, logs, prior)

        size = q.shape[0] // 2
        low, high = slice(0, size), slice(size, 2 * size)
        first = scores(low)
        second = scores(high)
        reduce(low, first)
        reduce(high, second)

    for (start, count), pair_ref in zip(groups, pairs):
        pl.when((at >= start) & (at < start + count))(functools.partial(work, pair_ref))

    @pl.when(at == heads)
    def _():
        send_ref[0] = send_logs(log_ref[...])


def text_partial(scal, valid, query_text, mine, pairs, groups, key_text, value_text):
    _, heads, time_tiles, _, _, _ = mine.shape
    text = query_text.shape[0]
    block = (2, 1, time_tiles, 2, VOL, HD)

    def of_group(start, count):
        return pl.BlockSpec(block, lambda i, s: (0, jnp.clip(i - start, 0, count - 1), 0, 0, 0, 0))

    word = pl.BlockSpec((text, HD), lambda i, s: (0, s[4] * heads + jnp.minimum(i, heads - 1)))
    return pl.pallas_call(
        functools.partial(text_body, groups),
        grid_spec=pltpu.PrefetchScalarGridSpec(
            num_scalar_prefetch=1,
            grid=(heads + 1,),
            in_specs=[pl.BlockSpec((1, text), lambda i, s: (0, 0)), word, of_group(0, heads), word, word]
            + [of_group(start, count) for start, count in groups],
            out_specs=[
                pl.BlockSpec((1, text, HD), lambda i, s: (jnp.minimum(i, heads - 1), 0, 0)),
                pl.BlockSpec((text, HD), lambda i, s: (0, 0)),
                pl.BlockSpec((1, text, HD), lambda i, s: (i, 0, 0)),
            ],
        ),
        out_shape=[
            jax.ShapeDtypeStruct((heads, text, HD), F32),
            jax.ShapeDtypeStruct((text, HD), F32),
            jax.ShapeDtypeStruct((heads + 1, text, HD), BF16),
        ],
        compiler_params=pltpu.CompilerParams(vmem_limit_bytes=VMEM),
        cost_estimate=cost(0),
        name="text",
    )(scal, valid, query_text, mine, key_text, value_text, *pairs)


def combine(parts, heads):
    logs = [part[1] for part in parts]
    top = functools.reduce(jnp.maximum, logs)
    weights = [jnp.exp(log - top) for log in logs]
    total = functools.reduce(jnp.add, weights)
    weights = [weight / total for weight in weights]
    outs = []
    for head in range(heads):
        terms = [weight[:, head : head + 1] * part[0](head) for weight, part in zip(weights, parts)]
        outs.append(functools.reduce(jnp.add, terms))
    return outs, top + jnp.log(total)


def join_body(sum_ref, log_ref, got_ref, out_ref):
    heads = sum_ref.shape[0]
    own = (lambda head: sum_ref[head], log_ref[...])
    got = (lambda head: got_ref[head].astype(F32), read_logs(got_ref[heads]))
    outs, logs = combine([own, got], heads)
    for head in range(heads):
        out_ref[head] = outs[head].astype(BF16)
    out_ref[heads] = send_logs(logs)


def join(sums, logs, got):
    return pl.pallas_call(
        join_body,
        out_shape=jax.ShapeDtypeStruct(got.shape, BF16),
        compiler_params=pltpu.CompilerParams(vmem_limit_bytes=VMEM),
        cost_estimate=cost(0),
        name="join",
    )(sums, logs, got)


def finish_body(scal, own_ref, got_ref, out_ref):
    heads = own_ref.shape[0] - 1
    low = scal[5] > 0
    parts = []
    for flag in (low, jnp.logical_not(low)):

        def pick(index, flag=flag):
            return jnp.where(flag, own_ref[index].astype(F32), got_ref[index].astype(F32))

        parts.append((pick, read_logs(pick(heads))))
    outs, _ = combine(parts, heads)
    for head in range(heads):
        out_ref[:, head * HD : (head + 1) * HD] = outs[head].astype(BF16)


def finish(scal, own, got):
    heads, text, _ = own.shape
    return pl.pallas_call(
        finish_body,
        grid_spec=pltpu.PrefetchScalarGridSpec(
            num_scalar_prefetch=1,
            grid=(1,),
            in_specs=[pl.BlockSpec(own.shape, lambda i, s: (0, 0, 0))] * 2,
            out_specs=pl.BlockSpec((text, (heads - 1) * HD), lambda i, s: (0, 0)),
        ),
        out_shape=jax.ShapeDtypeStruct((text, (heads - 1) * HD), BF16),
        compiler_params=pltpu.CompilerParams(vmem_limit_bytes=VMEM),
        cost_estimate=cost(0),
        name="finish",
    )(scal, own, got)


def after(value, *others):
    return lax.optimization_barrier((value, *others))[0]


def shards(query_video, key_video, value_video, query_text, key_text, value_text, text_valid):
    features = query_video.shape[3]
    heads = features // HD
    strips = lax.axis_size("tm")
    strip = lax.axis_index("tm")
    half = lax.axis_index("height")
    half_heads = heads // 2

    def swap(array):
        return lax.ppermute(array, "height", [(0, 1), (1, 0)])

    up = [(i, i + 1) for i in range(strips - 1)]
    down = [(i + 1, i) for i in range(strips - 1)]
    scal = jnp.stack(
        [1 - half, strip > 0, strip < strips - 1, strip == 0, half, strip < strips // 2]
    ).astype(jnp.int32)
    valid = text_valid.reshape(1, -1)
    groups = head_groups(half_heads)

    def to_neighbours(array):
        return lax.ppermute(array, "tm", up), lax.ppermute(array, "tm", down)

    (mine,) = pack_half(scal, key_video, value_video, (half_heads,))
    mine_sides = to_neighbours(mine)
    theirs = pack_half(after(scal, mine), key_video, value_video, [count for _, count in groups], query_video)
    pairs = [swap(array) for array in theirs[:-1]]
    pair_query = swap(theirs[-1])
    sums, logs, sent = text_partial(after(scal, pair_query), valid, query_text, mine, pairs, groups, key_text, value_text)

    middle = strips // 2
    for step in range(1, middle):
        got = lax.ppermute(sent, "tm", [(step - 1, step), (strips - step, strips - step - 1)])
        sent = join(sums, after(logs, *mine_sides), got)
    got = lax.ppermute(sent, "tm", [(middle - 1, middle), (middle, middle - 1)])

    outs = ()
    for index, (start, count) in enumerate(groups):
        pair = (pairs[index], *to_neighbours(after(pairs[index], sent) if index else pairs[index]))
        outs = video_group(
            scal, valid, query_video, pair_query, (mine, *mine_sides), pair, key_text, value_text, outs, start, count
        )
        if index == 0:
            opened = after(scal, outs[0])
    column = (1 - half) * half_heads * HD
    out_video = lax.dynamic_update_slice_in_dim(outs[0], swap(outs[1]), column, 3)

    done = finish(opened, sent, got)
    for step in range(middle - 1, 0, -1):
        got = lax.ppermute(done, "tm", [(step, step - 1), (strips - step - 1, strips - step)])
        done = jnp.where((strip == step - 1) | (strip == strips - step), after(got, outs[1]), done)
    other = swap(done)
    first = half == 0
    out_text = jnp.concatenate([jnp.where(first, done, other), jnp.where(first, other, done)], axis=1)
    return (out_video, out_text)


def solution(mesh):
    if mesh.shape["height"] != 2 or mesh.shape["tm"] % 2:
        raise ValueError("unsupported mesh")
    placed = (
        P("grp", "height", "tm", "head"),
        P("grp", "height", "tm", "head"),
        P("grp", "height", "tm", "head"),
        P("grp", "head"),
        P("grp", "head"),
        P("grp", "head"),
        P("grp"),
    )
    return jax.shard_map(
        shards,
        mesh=mesh,
        in_specs=placed,
        out_specs=(P("grp", "height", "tm", "head"), P("grp", "head")),
        check_vma=False,
    )
```

```python
import functools
import math

import jax
import jax.numpy as jnp
from jax import lax
from jax.experimental import pallas as pl
from jax.experimental.pallas import tpu as pltpu
from jax.sharding import PartitionSpec as P

HD = 128
TILE = 4
VOL = TILE**3
BF16 = jnp.bfloat16
F32 = jnp.float32
SCALE = 1.0 / math.sqrt(HD)
SCALE_2 = SCALE * math.log2(math.e)
VMEM = 255 << 18
THIRD = 32
SIZES = (3, 3)


def cost(microseconds):
    return pl.CostEstimate(flops=int(microseconds * 1.15e9), bytes_accessed=1, transcendentals=0)


def head_groups(heads):
    sizes = SIZES if heads == sum(SIZES) else [heads - 1, 1]
    starts = [sum(sizes[:i]) for i in range(len(sizes))]
    return list(zip(starts, sizes))


def dot_nt(a, b):
    return lax.dot_general(a, b, (((1,), (1,)), ((), ())), preferred_element_type=F32)


def dot_nn(a, b):
    return lax.dot_general(a, b, (((1,), (0,)), ((), ())), preferred_element_type=F32)


def weigh(p, v):
    return dot_nn(p.astype(BF16), jnp.concatenate([v, jnp.ones_like(v)], axis=1))


def pack_body(sizes, scal, *rest):
    k_ref, v_ref = rest[:2]
    tiles = rest[-len(sizes) - 1 : -1] if len(rest) == len(sizes) + 4 else rest[-len(sizes) :]
    head = 0
    for size, kv_ref in zip(sizes, tiles):
        for at in range(size):
            lanes = slice(head * HD, (head + 1) * HD)
            head += 1
            for which, ref in enumerate((k_ref, v_ref)):
                for t in range(ref.shape[0] // TILE):
                    frames = slice(t * TILE, (t + 1) * TILE)
                    for r in range(ref.shape[1] // TILE):
                        tile = ref[frames, r * TILE : (r + 1) * TILE, :, lanes]
                        kv_ref[which, at, t, r] = tile.reshape(VOL, HD)
    if len(rest) == len(sizes) + 4:
        rest[-1][...] = rest[2][...]


def pack_half(scal, key_video, value_video, sizes, query_video=None):
    frames, rows, cols, features = key_video.shape
    time_tiles = frames // TILE
    row_tiles = rows // TILE
    theirs = query_video is not None
    depth = 2 if time_tiles % 2 == 0 else 1
    block = pl.BlockSpec(
        (depth * TILE, rows, cols, features // 2), lambda t, s: (t, 0, 0, 1 - s[4] if theirs else s[4])
    )
    operands = [key_video, value_video]
    out_specs = [
        pl.BlockSpec((2, size, depth, row_tiles, VOL, HD), lambda t, s: (0, 0, t, 0, 0, 0)) for size in sizes
    ]
    out_shape = [jax.ShapeDtypeStruct((2, size, time_tiles, row_tiles, VOL, HD), BF16) for size in sizes]
    if theirs:
        operands.append(query_video)
        out_specs.append(pl.BlockSpec((depth * TILE, rows, cols, features // 2), lambda t, s: (t, 0, 0, 0)))
        out_shape.append(jax.ShapeDtypeStruct((frames, rows, cols, features // 2), BF16))
    return pl.pallas_call(
        functools.partial(pack_body, sizes),
        grid_spec=pltpu.PrefetchScalarGridSpec(
            num_scalar_prefetch=1, grid=(time_tiles // depth,), in_specs=[block] * len(operands), out_specs=out_specs
        ),
        out_shape=out_shape,
        compiler_params=pltpu.CompilerParams(vmem_limit_bytes=VMEM),
        cost_estimate=cost(0),
        name="pack",
    )(scal, *operands)


def video_body(scal, valid_ref, own_q, pair_q, *rest):
    own_tiles, pair_tiles, (tk_ref, tv_ref) = rest[:3], rest[3:6], rest[6:8]
    own_out, pair_out = rest[-2:]
    has_left = scal[1] > 0
    has_right = scal[2] > 0
    time_tiles = own_q.shape[0] // TILE
    open_keys = valid_ref[...] > 0

    def load(ref, which, first, last, row):
        picked = ref[which, 0, first:last] if row is None else ref[which, 0, first:last, pl.ds(row, 1)]
        return picked.reshape(picked.shape[0] * picked.shape[1] * VOL, HD)

    def scores(step):
        part, t = step
        q_ref = (own_q, pair_q)[part]
        near = scal[0] if part == 0 else 1 - scal[0]
        far_rows = pl.ds((1 - near) * TILE, TILE)
        near_rows = pl.ds(near * TILE, TILE)
        own, left, right = (own_tiles, pair_tiles)[part]
        edge, edge_left, edge_right = (pair_tiles, own_tiles)[part]
        row = 1 - near
        first = max(t - 1, 0)
        last = min(t + 1, time_tiles - 1) + 1
        frames = slice(t * TILE, (t + 1) * TILE)
        q_far = q_ref[frames, far_rows, :, :].reshape(VOL, HD)
        q_near = q_ref[frames, near_rows, :, :].reshape(VOL, HD)
        q_all = jnp.concatenate([q_far, q_near], axis=0)
        s_text = jnp.where(open_keys, dot_nt(q_all, tk_ref[...]), -jnp.inf)
        wide = [(s_text, None, None)]
        for ref, ok in ((own, None), (left, has_left), (right, has_right)):
            wide.append((dot_nt(q_all, load(ref, 0, first, last, None)), ref, ok))
        thin = []
        for ref, ok in ((edge, None), (edge_left, has_left), (edge_right, has_right)):
            thin.append((dot_nt(q_near, load(ref, 0, first, last, row)), ref, ok))
        return first, last, wide, thin, row, far_rows, near_rows

    def peak(entries):
        tops = {}
        for s, _, ok in entries:
            local = {}
            for at in range(0, s.shape[1], HD):
                piece = s[:, at : at + HD]
                width = piece.shape[1]
                local[width] = jnp.maximum(local[width], piece) if width in local else piece
            for width, top in local.items():
                top = top if ok is None else jnp.where(ok, top, -jnp.inf)
                tops[width] = jnp.maximum(tops[width], top) if width in tops else top
        return functools.reduce(jnp.maximum, [jnp.max(top, axis=1, keepdims=True) for top in tops.values()])

    def gather(entries, m, first, last, row):
        summed = None
        for s, ref, ok in entries:
            base = m if ok is None else jnp.where(ok, m, jnp.inf)
            v = tv_ref[...] if ref is None else load(ref, 1, first, last, row)
            part = weigh(jnp.exp2((s - base) * SCALE_2), v)
            summed = part if summed is None else summed + part
        return summed

    def finish(step, state):
        part, t = step
        out_ref = (own_out, pair_out)[part]
        first, last, wide, thin, row, far_rows, near_rows = state
        frames = slice(t * TILE, (t + 1) * TILE)
        m_all = peak(wide)
        m_near = jnp.maximum(m_all[VOL:], peak(thin))
        m_all = jnp.concatenate([m_all[:VOL], m_near], axis=0)
        summed = gather(wide, m_all, first, last, None)
        far = summed[:VOL]
        close = summed[VOL:] + gather(thin, m_near, first, last, row)
        for rows, value in ((far_rows, far), (near_rows, close)):
            out = value[:, :HD] / value[:, HD:]
            out_ref[frames, rows, :, :] = out.astype(BF16).reshape(TILE, TILE, TILE, HD)

    steps = [(part, t) for part in range(2) for t in range(time_tiles)]
    state = scores(steps[0])
    for at, step in enumerate(steps):
        following = scores(steps[at + 1]) if at + 1 < len(steps) else None
        finish(step, state)
        state = following


def video_group(scal, valid, query_video, pair_query, mine, pair, key_text, value_text, prior, start, count):
    frames, rows, cols, _ = query_video.shape
    half_heads = pair_query.shape[3] // HD
    time_tiles = frames // TILE
    text = key_text.shape[0]
    block = (frames, rows, cols, HD)
    own_head = pl.BlockSpec(block, lambda i, s: (0, 0, 0, s[4] * half_heads + start + i))
    pair_head = pl.BlockSpec(block, lambda i, s: (0, 0, 0, start + i))
    of_half = pl.BlockSpec((2, 1, time_tiles, 2, VOL, HD), lambda i, s: (0, start + i, 0, 0, 0, 0))
    of_group = pl.BlockSpec((2, 1, time_tiles, 2, VOL, HD), lambda i, s: (0, i, 0, 0, 0, 0))
    word = pl.BlockSpec((text, HD), lambda i, s: (0, s[4] * half_heads + start + i))
    specs = [pl.BlockSpec((1, text), lambda i, s: (0, 0)), own_head, pair_head]
    specs += [of_half] * 3 + [of_group] * 3 + [word, word]
    operands = [scal, valid, query_video, pair_query, *mine, *pair, key_text, value_text]
    aliases = {}
    for at, array in enumerate(prior):
        specs.append(pl.BlockSpec(memory_space=pl.ANY))
        aliases[len(operands)] = at
        operands.append(array)
    return pl.pallas_call(
        video_body,
        grid_spec=pltpu.PrefetchScalarGridSpec(
            num_scalar_prefetch=1,
            grid=(count,),
            in_specs=specs,
            out_specs=[own_head, pair_head],
        ),
        out_shape=[
            jax.ShapeDtypeStruct(query_video.shape, BF16),
            jax.ShapeDtypeStruct(pair_query.shape, BF16),
        ],
        input_output_aliases=aliases,
        compiler_params=pltpu.CompilerParams(vmem_limit_bytes=VMEM),
        cost_estimate=cost(0),
        name="video",
    )(*operands)


def lane_of(shape):
    return lax.broadcasted_iota(jnp.int32, shape, len(shape) - 1)


def send_logs(logs):
    high = logs.astype(BF16).astype(F32)
    mid = (logs - high).astype(BF16).astype(F32)
    low = logs - high - mid
    lane = lane_of(logs.shape)
    whole = jnp.where(lane < THIRD, high, 0.0)
    whole = jnp.where((lane >= THIRD) & (lane < 2 * THIRD), pltpu.roll(mid, THIRD, 1), whole)
    whole = jnp.where((lane >= 2 * THIRD) & (lane < 3 * THIRD), pltpu.roll(low, 2 * THIRD, 1), whole)
    return jnp.where(lane == HD - 1, 1.0, whole).astype(BF16)


def read_logs(sent):
    whole = sent.astype(F32)
    logs = whole + pltpu.roll(whole, HD - THIRD, 1) + pltpu.roll(whole, HD - 2 * THIRD, 1)
    return jnp.where(whole[:, HD - 1 :] > 0, logs, -jnp.inf)


def text_body(groups, scal, valid_ref, q_ref, mine_ref, tk_ref, tv_ref, *rest):
    pairs = rest[: len(groups)]
    sum_ref, log_ref, send_ref = rest[len(groups) :]
    at = pl.program_id(0)
    heads = pl.num_programs(0) - 1

    def work(pair_ref):
        q = q_ref[...]

        def tokens(ref, which):
            whole = ref[which, 0]
            return whole.reshape(whole.shape[0] * whole.shape[1] * VOL, HD)

        def scores(rows):
            near = jnp.where((valid_ref[...] > 0) & (scal[3] > 0), dot_nt(q[rows], tk_ref[...]), -jnp.inf)
            return [dot_nt(q[rows], tokens(mine_ref, 0)), dot_nt(q[rows], tokens(pair_ref, 0)), near]

        def reduce(rows, parts):
            m = functools.reduce(jnp.maximum, [jnp.max(s, axis=1, keepdims=True) for s in parts])
            values = (tokens(mine_ref, 1), tokens(pair_ref, 1), tv_ref[...])
            both = functools.reduce(
                jnp.add, [weigh(jnp.exp2((s - m) * SCALE_2), v) for s, v in zip(parts, values)]
            )
            total = both[:, HD:]
            out = both[:, :HD] / total
            sum_ref[0, rows] = out
            send_ref[0, rows] = out.astype(BF16)
            logs = m * SCALE + jnp.log(total)
            prior = jnp.where(at == 0, 0.0, log_ref[rows])
            log_ref[rows] = jnp.where(lane_of(logs.shape) == at, logs, prior)

        size = q.shape[0] // 2
        low, high = slice(0, size), slice(size, 2 * size)
        first = scores(low)
        second = scores(high)
        reduce(low, first)
        reduce(high, second)

    for (start, count), pair_ref in zip(groups, pairs):
        pl.when((at >= start) & (at < start + count))(functools.partial(work, pair_ref))

    @pl.when(at == heads)
    def _():
        send_ref[0] = send_logs(log_ref[...])


def text_partial(scal, valid, query_text, mine, pairs, groups, key_text, value_text):
    _, heads, time_tiles, _, _, _ = mine.shape
    text = query_text.shape[0]
    block = (2, 1, time_tiles, 2, VOL, HD)

    def of_group(start, count):
        return pl.BlockSpec(block, lambda i, s: (0, jnp.clip(i - start, 0, count - 1), 0, 0, 0, 0))

    word = pl.BlockSpec((text, HD), lambda i, s: (0, s[4] * heads + jnp.minimum(i, heads - 1)))
    return pl.pallas_call(
        functools.partial(text_body, groups),
        grid_spec=pltpu.PrefetchScalarGridSpec(
            num_scalar_prefetch=1,
            grid=(heads + 1,),
            in_specs=[pl.BlockSpec((1, text), lambda i, s: (0, 0)), word, of_group(0, heads), word, word]
            + [of_group(start, count) for start, count in groups],
            out_specs=[
                pl.BlockSpec((1, text, HD), lambda i, s: (jnp.minimum(i, heads - 1), 0, 0)),
                pl.BlockSpec((text, HD), lambda i, s: (0, 0)),
                pl.BlockSpec((1, text, HD), lambda i, s: (i, 0, 0)),
            ],
        ),
        out_shape=[
            jax.ShapeDtypeStruct((heads, text, HD), F32),
            jax.ShapeDtypeStruct((text, HD), F32),
            jax.ShapeDtypeStruct((heads + 1, text, HD), BF16),
        ],
        compiler_params=pltpu.CompilerParams(vmem_limit_bytes=VMEM),
        cost_estimate=cost(0),
        name="text",
    )(scal, valid, query_text, mine, key_text, value_text, *pairs)


def combine(parts, heads):
    logs = [part[1] for part in parts]
    top = functools.reduce(jnp.maximum, logs)
    weights = [jnp.exp(log - top) for log in logs]
    total = functools.reduce(jnp.add, weights)
    weights = [weight / total for weight in weights]
    outs = []
    for head in range(heads):
        terms = [weight[:, head : head + 1] * part[0](head) for weight, part in zip(weights, parts)]
        outs.append(functools.reduce(jnp.add, terms))
    return outs, top + jnp.log(total)


def join_body(sum_ref, log_ref, got_ref, out_ref):
    heads = sum_ref.shape[0]
    own = (lambda head: sum_ref[head], log_ref[...])
    got = (lambda head: got_ref[head].astype(F32), read_logs(got_ref[heads]))
    outs, logs = combine([own, got], heads)
    for head in range(heads):
        out_ref[head] = outs[head].astype(BF16)
    out_ref[heads] = send_logs(logs)


def join(sums, logs, got):
    return pl.pallas_call(
        join_body,
        out_shape=jax.ShapeDtypeStruct(got.shape, BF16),
        compiler_params=pltpu.CompilerParams(vmem_limit_bytes=VMEM),
        cost_estimate=cost(0),
        name="join",
    )(sums, logs, got)


def finish_body(scal, own_ref, got_ref, out_ref):
    heads = own_ref.shape[0] - 1
    low = scal[5] > 0
    parts = []
    for flag in (low, jnp.logical_not(low)):

        def pick(index, flag=flag):
            return jnp.where(flag, own_ref[index], got_ref[index]).astype(F32)

        parts.append((pick, read_logs(pick(heads))))
    outs, _ = combine(parts, heads)
    for head in range(heads):
        out_ref[:, head * HD : (head + 1) * HD] = outs[head].astype(BF16)


def finish(scal, own, got):
    heads, text, _ = own.shape
    return pl.pallas_call(
        finish_body,
        grid_spec=pltpu.PrefetchScalarGridSpec(
            num_scalar_prefetch=1,
            grid=(1,),
            in_specs=[pl.BlockSpec(own.shape, lambda i, s: (0, 0, 0))] * 2,
            out_specs=pl.BlockSpec((text, (heads - 1) * HD), lambda i, s: (0, 0)),
        ),
        out_shape=jax.ShapeDtypeStruct((text, (heads - 1) * HD), BF16),
        compiler_params=pltpu.CompilerParams(vmem_limit_bytes=VMEM),
        cost_estimate=cost(0),
        name="finish",
    )(scal, own, got)


def after(value, *others):
    return lax.optimization_barrier((value, *others))[0]


def shards(query_video, key_video, value_video, query_text, key_text, value_text, text_valid):
    features = query_video.shape[3]
    heads = features // HD
    strips = lax.axis_size("tm")
    strip = lax.axis_index("tm")
    half = lax.axis_index("height")
    half_heads = heads // 2

    def swap(array):
        return lax.ppermute(array, "height", [(0, 1), (1, 0)])

    up = [(i, i + 1) for i in range(strips - 1)]
    down = [(i + 1, i) for i in range(strips - 1)]
    scal = jnp.stack(
        [1 - half, strip > 0, strip < strips - 1, strip == 0, half, strip < strips // 2]
    ).astype(jnp.int32)
    valid = text_valid.reshape(1, -1)
    groups = head_groups(half_heads)

    def to_neighbours(array):
        return lax.ppermute(array, "tm", up), lax.ppermute(array, "tm", down)

    (mine,) = pack_half(scal, key_video, value_video, (half_heads,))
    mine_sides = to_neighbours(mine)
    theirs = pack_half(after(scal, mine), key_video, value_video, [count for _, count in groups], query_video)
    pairs = [swap(array) for array in theirs[:-1]]
    pair_query = swap(theirs[-1])
    sums, logs, sent = text_partial(after(scal, pair_query), valid, query_text, mine, pairs, groups, key_text, value_text)

    middle = strips // 2
    for step in range(1, middle):
        got = lax.ppermute(sent, "tm", [(step - 1, step), (strips - step, strips - step - 1)])
        sent = join(sums, after(logs, *mine_sides), got)
    got = lax.ppermute(sent, "tm", [(middle - 1, middle), (middle, middle - 1)])

    outs = ()
    for index, (start, count) in enumerate(groups):
        pair = (pairs[index], *to_neighbours(after(pairs[index], sent) if index else pairs[index]))
        outs = video_group(
            scal, valid, query_video, pair_query, (mine, *mine_sides), pair, key_text, value_text, outs, start, count
        )
        if index == 0:
            opened = after(scal, outs[0])
    column = (1 - half) * half_heads * HD
    out_video = lax.dynamic_update_slice_in_dim(outs[0], swap(outs[1]), column, 3)

    done = finish(opened, sent, got)
    for step in range(middle - 1, 0, -1):
        got = lax.ppermute(done, "tm", [(step, step - 1), (strips - step - 1, strips - step)])
        done = jnp.where((strip == step - 1) | (strip == strips - step), after(got, outs[1]), done)
    other = swap(done)
    first = half == 0
    out_text = jnp.concatenate([jnp.where(first, done, other), jnp.where(first, other, done)], axis=1)
    return (out_video, out_text)


def solution(mesh):
    if mesh.shape["height"] != 2 or mesh.shape["tm"] % 2:
        raise ValueError("unsupported mesh")
    placed = (
        P("grp", "height", "tm", "head"),
        P("grp", "height", "tm", "head"),
        P("grp", "height", "tm", "head"),
        P("grp", "head"),
        P("grp", "head"),
        P("grp", "head"),
        P("grp"),
    )
    return jax.shard_map(
        shards,
        mesh=mesh,
        in_specs=placed,
        out_specs=(P("grp", "height", "tm", "head"), P("grp", "head")),
        check_vma=False,
    )
```
